512 devices in a mesh: gx: 32 (over y_hi, z), az: 4 (over y_lo, core), ta: 4 (over x).
Axes of the slice: x: 4, y: 8 (y_hi: 4, y_lo: 2; y = y_hi * 2 + y_lo), z: 8, core: 2. Of those that a mesh axis runs over, the one named last changes fastest.
Arguments:
- velocity: float32 [512, 32, 1024], P('gx', 'az', 'ta'), may hold values from -6 to 6
- pressure: float32 [512, 32, 1024], P('gx', 'az', 'ta'), may hold values from -6 to 6
- offsets: int32 [8], replicated, may hold values from 1 to 16, as said below
Outputs:
- correlation: float32 [512, 8, 1056], P(('gx', 'az', 'ta'))
The draws below stay inside these ranges and needn't reach their ends.
Inputs may be any that keep to these rules, and one draw needn't show every extreme that they name: `offsets`: the 8 separations are distinct and the largest equals 16.
All inputs are finite; a program needn't handle non-finite values.
Results may differ from the reference program's by a relative error of at most 0.00007.
Values sent between devices are 32-bit elements; how exact they have to be, the bound alone decides.
A program may use at most 64 MiB of HBM per device.

```python
import math
import jax
import jax.numpy as jnp
from jax import lax

AZIM = 32
NBR = 8
SPAN = 16
MAXLAG = 16
LAGS = 33
STATIONS = 512
TIMES = 1024


def draw_offsets(key, part):
    shuffled = jax.random.permutation(key, SPAN - 1).astype(jnp.int32) + 1
    largest = jnp.full((1,), SPAN, jnp.int32)
    return jnp.concatenate([shuffled[:NBR - 1], largest]).astype(jnp.int32)


def steps_of(own_key, dims, shards, least, high):
    factor_of, own = 1.0, jax.random.fold_in(own_key, 6)
    for position, blocks in shards:
        steps = jnp.exp(jax.random.uniform(jax.random.fold_in(own, position), (blocks,), jnp.float32, least / len(shards), high / len(shards)))
        factor_of = factor_of * jnp.repeat(steps, dims[position] // blocks).reshape([-1 if axis == position else 1 for axis in range(len(dims))])
    return factor_of


def scatter_about(rng, shape, width, most, shards=(), kind=jnp.bfloat16):
    entries = jax.random.normal(rng, shape, jnp.float32) * width
    if len(shards) > 0:
        entries = steps_of(rng, shape, shards, -0.22, 0.18) * entries
    return jnp.clip(entries, min=-most, max=most).astype(kind)


def setup_inputs(seed: int = 0) -> dict:
    arg_keys = jax.random.split(jax.random.key(seed), 4)
    return {
        "velocity": scatter_about(arg_keys[0], (STATIONS, AZIM, TIMES), 1.0, 6.0, ((0, 32), (1, 4), (2, 4)), jnp.float32),
        "pressure": scatter_about(arg_keys[1], (STATIONS, AZIM, TIMES), 1.0, 6.0, ((0, 32), (1, 4), (2, 4)), jnp.float32),
        "offsets": draw_offsets(jax.random.fold_in(arg_keys[3], 71), 0),
    }


def reference(velocity, pressure, offsets):
    length = 2 * TIMES
    factor = 1.0 / math.sqrt(TIMES * AZIM)
    vel_hat = jnp.fft.rfft2(velocity, s=(AZIM, length), axes=(1, 2))
    pres_ext = jnp.concatenate([pressure, jnp.zeros((SPAN, AZIM, TIMES), pressure.dtype)], axis=0)
    pres_hat = jnp.fft.rfft2(pres_ext, s=(AZIM, length), axes=(1, 2))

    def one_station(station):
        own_hat = jnp.conj(lax.dynamic_index_in_dim(vel_hat, station, 0, keepdims=False))
        partners = jnp.take(pres_hat, station + offsets, axis=0)
        inverse = jnp.fft.irfft2(own_hat[None] * partners, s=(AZIM, length), axes=(1, 2))
        window = jnp.concatenate([inverse[:, :, length - MAXLAG:], inverse[:, :, :MAXLAG + 1]], axis=2)
        return jnp.transpose(window, (0, 2, 1)).reshape(NBR, LAGS * AZIM) * factor
    result = lax.map(one_station, jnp.arange(STATIONS, dtype=jnp.int32))
    return result.astype(jnp.float32)
```

```python
import math

import jax
import jax.numpy as jnp
import numpy as np
from jax import lax
from jax.experimental import pallas as pl
from jax.experimental.pallas import tpu as pltpu
from jax.sharding import PartitionSpec as P

AZIM = 32
NBR = 8
MAXLAG = 16
LAGS = 33
MODES = 24
LEN = 128
ROWS = 72
MESH = pl.DeviceIdType.MESH
F32, BF16 = jnp.float32, jnp.bfloat16


def halves(table):
    high = table.astype(BF16)
    return high, (table - high.astype(np.float32)).astype(BF16)


def tables():
    mode, azim = np.arange(MODES), np.arange(AZIM)
    angle = 2 * np.pi * ((mode[:, None] * azim[None, :]) % AZIM) / AZIM
    parts = np.stack([np.cos(angle), np.sin(angle)])
    parts[1, 0], parts[1, 16] = 0, 0
    parts[:, 17:] = 0
    eye = np.eye(8)

    def over_stations(part):
        full = np.einsum("st,cmq->csmtq", eye, part)
        return full.reshape(2 * 8 * MODES, 8 * part.shape[2]).astype(np.float32)

    def left(table):
        high, low = halves(table)
        return np.concatenate([high, high, low], axis=1)

    def right(table):
        high, low = halves(table)
        return np.concatenate([high, high, low], axis=0)

    t = np.arange(LEN)
    omega = 2 * np.pi * ((t[:, None] * t[None, :]) % LEN) / LEN
    cos, sin = np.cos(omega), np.sin(omega)
    time = np.block([[cos, -sin], [-sin, -cos]]).astype(np.float32)
    lag = np.arange(-MAXLAG, MAXLAG + 1)
    omega = 2 * np.pi * ((lag[:, None] * t[None, :]) % LEN) / LEN
    cos, sin = np.cos(omega) / LEN, np.sin(omega) / LEN
    back = np.zeros((ROWS, 2 * LEN), np.float32)
    back[: 2 * LAGS] = np.block([[cos, -sin], [sin, cos]])
    slot = np.arange(16)
    angle = 2 * np.pi * ((slot[:, None] * azim[None, :]) % AZIM) / AZIM
    real, imag = 2 * np.cos(angle), -2 * np.sin(angle)
    real[0], imag[0] = 1, np.where(azim % 2 == 0, 1, -1)
    scale = 1.0 / (AZIM * math.sqrt(AZIM * 1024))
    last = np.concatenate([np.kron(eye, real), np.kron(eye, imag)], axis=1) * scale
    return (
        left(over_stations(parts)),
        left(over_stations(parts[:, :, :16])),
        right(time),
        left(back),
        right(last.astype(np.float32)),
    )


def split(value):
    high = value.astype(BF16)
    return high, (value - high.astype(F32)).astype(BF16)


def as_left(value):
    high, low = split(value)
    return jnp.concatenate([high, low, high], axis=1)


def as_right(value):
    high, low = split(value)
    return jnp.concatenate([high, low, high], axis=0)


def dot(left, right):
    return lax.dot_general(left, right, (((1,), (0,)), ((), ())), preferred_element_type=F32)


def lanes_of(shape):
    return lax.broadcasted_iota(jnp.int32, shape, len(shape) - 1)


def kernel(
    groups, vel, pres, offs, t_av, t_ap, t_w, t_wi, t_b, out,
    vbuf, pbuf, vraw, pack, hal, av, ap, w, wi, b, fv, fp, part, recv, rows_buf, turn_buf,
    local_sem, send_sem, vrecv, precv, zrecv, relay, hrecv, send2, recv2,
):
    gx, az, ta = lax.axis_index("gx"), lax.axis_index("az"), lax.axis_index("ta")
    y, c = az // 2, az % 2
    other = 1 - c
    partner = {"gx": gx, "az": 2 * y + other, "ta": ta}
    up = lax.rem(gx + groups - 1, groups)
    down = lax.rem(gx + 1, groups)
    mine = pl.ds(pl.multiple_of(az * 8, 8), 8)
    own_q = pl.ds(pl.multiple_of(c * 8, 8), 8)

    def device(a, t, g=gx):
        return (g, a, t)

    barrier = pltpu.get_barrier_semaphore()
    for step in range(1, 16):
        spot = lax.rem(az * 4 + ta + step, 16)
        pl.semaphore_signal(
            barrier, inc=1, device_id=device(spot // 4, spot % 4), device_id_type=MESH
        )

    for near in (up, down):
        pl.semaphore_signal(barrier, inc=1, device_id=device(az, ta, near), device_id_type=MESH)

    here = [
        pltpu.make_async_copy(vel, vraw, local_sem.at[0]),
        pltpu.make_async_copy(vel.at[pl.ds(8 * c, 8)], vbuf.at[:, mine], local_sem.at[1]),
        pltpu.make_async_copy(pres, pbuf.at[pl.ds(0, 16), own_q], local_sem.at[2]),
    ]
    for number, (source, target) in enumerate(
        [(t_av, av), (t_ap, ap), (t_w, w), (t_wi, wi), (t_b, b)]
    ):
        here.append(pltpu.make_async_copy(source, target, local_sem.at[3 + number]))
    for copy in here:
        copy.start()
    here[0].wait()

    lane8 = lanes_of((8, 128))
    for half in range(2):
        right = jnp.zeros((8, 128), F32)
        left = jnp.zeros((8, 128), F32)
        for j in range(8):
            here_lane = lane8 // 16 == j
            last = vraw[8 * half + j, :, 128:256]
            first = vraw[8 * half + j, :, 0:128]
            right = jnp.where(here_lane, pltpu.roll(last, (16 * j + 16) % 128, 1), right)
            left = jnp.where(here_lane, pltpu.roll(first, 16 * j, 1), left)
        pack[0, half] = right
        pack[1, half] = left

    pl.semaphore_wait(barrier, 17)

    def remote(source, target, send, receive, to):
        return pltpu.make_async_remote_copy(
            src_ref=source, dst_ref=target, send_sem=send, recv_sem=receive,
            device_id=to, device_id_type=MESH,
        )

    halo = [
        remote(
            pres.at[pl.ds(8 * n, 8)], pbuf.at[pl.ds(16 + 8 * n, 8), own_q],
            send_sem.at[n], zrecv.at[n], device(az, ta, up),
        )
        for n in range(2)
    ]

    @pl.when(gx > 0)
    def _():
        for copy in halo:
            copy.start()

    own_half = vel.at[pl.ds(8 * c, 8)]
    other_half = vel.at[pl.ds(8 * other, 8)]
    sends = [
        remote(own_half, vbuf.at[:, mine], send_sem.at[2], vrecv.at[0],
               device(2 * (1 - y) + c, ta)),
        remote(other_half, vbuf.at[:, mine], send_sem.at[3], vrecv.at[1],
               device(2 * (1 - y) + other, ta)),
        remote(other_half, vbuf.at[:, mine], send_sem.at[4], vrecv.at[2],
               device(2 * y + other, ta)),
        remote(pres, pbuf.at[pl.ds(0, 16), own_q], send_sem.at[5], precv.at[0],
               device(2 * y + other, ta)),
    ]
    for a in range(4):
        for side, shift in ((0, 1), (1, 3)):
            sends.append(
                remote(pack.at[side, a % 2], hal.at[side, mine],
                       send_sem.at[6 + 2 * a + side], hrecv.at[side, az],
                       device(a, lax.rem(ta + shift, 4)))
            )
    for copy in sends:
        copy.start()

    for copy in here[3:]:
        copy.wait()
    here[2].wait()
    sends[3].wait_recv()

    lane = lanes_of((384, 128))
    zero = jnp.zeros((384, 128), F32)

    def pressure(chunk):
        rows = pbuf[pl.ds(pl.multiple_of(8 * c + 8 * chunk, 8), 8)].reshape(128, 256)
        modes = dot(ap[...], as_right(rows))
        first, second = modes[:, :128], modes[:, 128:]
        windows = [
            jnp.where(lane < 96, first, zero),
            jnp.where(lane < 32, second, jnp.where(lane >= 96, first, zero)),
            jnp.where(lane >= 32, second, zero),
        ]
        for n, window in enumerate(windows):
            both = jnp.concatenate([window[:192], window[192:]], axis=1)
            spectrum = dot(as_left(both), w[...])
            fp[pl.ds(8 * chunk, 8), :, n * 256:(n + 1) * 256] = spectrum.reshape(8, MODES, 256)

    def velocity():
        lane = lanes_of((32, 128))
        low = jnp.where(ta > 0, hal[0], 0.0)
        high = jnp.where(ta < 3, hal[1], 0.0)
        columns = [[], [], []]
        for j in range(8):
            first, second = vbuf[j, :, 0:128], vbuf[j, :, 128:256]
            before = pltpu.roll(low, (112 - 16 * j) % 128, 1)
            after = pltpu.roll(high, (128 - 16 * j) % 128, 1)
            columns[0].append(jnp.where(lane < 112, first, before))
            columns[1].append(jnp.where(lane < 64, second, first))
            columns[2].append(jnp.where(lane >= 16, second, after))
        for n in range(3):
            rows = jnp.concatenate(columns[n], axis=0)
            modes = dot(av[...], as_right(rows))
            both = jnp.concatenate([modes[:192], modes[192:]], axis=1)
            spectrum = dot(as_left(both), w[...])
            fv[:, :, n * 256:(n + 1) * 256] = spectrum.reshape(8, MODES, 256)

    pressure(0)

    onward = [
        remote(
            pbuf.at[pl.ds(16 + 8 * n, 8), own_q], pbuf.at[pl.ds(16 + 8 * n, 8), own_q],
            send_sem.at[14 + n], relay.at[n], partner_id(gx, y, other, ta),
        )
        for n in range(2)
    ]

    here[1].wait()
    for copy in sends[:3]:
        copy.wait_recv()
    for side in range(2):
        for a in range(4):
            pltpu.make_async_copy(
                pack.at[0, 0], hal.at[side, pl.ds(8 * a, 8)], hrecv.at[side, a]
            ).wait()
    velocity()

    @pl.when(gx < groups - 1)
    def _():
        for n in range(2):
            halo[n].wait_recv()
            onward[n].start()
        for n in range(2):
            onward[n].wait_recv()

    @pl.when(gx == groups - 1)
    def _():
        pbuf[16:32] = jnp.zeros((16, 16, 256), F32)

    pressure(1)
    pressure(2)

    slot = 2 * ta + y

    def target_of(s):
        return device(2 * c + s // 4, s % 4)

    def outgoing(s):
        return remote(part.at[s], recv.at[slot], send2.at[s], recv2.at[slot], target_of(s))

    def deliver(s):
        to_self = jnp.logical_and(y == c, s == 4 * c + ta)

        @pl.when(to_self)
        def _():
            pltpu.make_async_copy(part.at[s], recv.at[slot], recv2.at[slot]).start()

        @pl.when(jnp.logical_not(to_self))
        def _():
            outgoing(s).start()

    def station(s, carry):
        v = [[fv[s, 8 * i:8 * i + 8, 128 * n:128 * n + 128] for n in range(6)] for i in range(3)]
        rows = []
        for k in range(NBR):
            near = s + offs[k]
            real, imag = [], []
            for i in range(3):
                re = im = None
                for n in range(3):
                    vr, vi = v[i][2 * n], v[i][2 * n + 1]
                    pr = fp[near, 8 * i:8 * i + 8, 256 * n:256 * n + 128]
                    pi = fp[near, 8 * i:8 * i + 8, 256 * n + 128:256 * n + 256]
                    one, two = vr * pr + vi * pi, vr * pi - vi * pr
                    re, im = (one, two) if n == 0 else (re + one, im + two)
                real.append(re)
                imag.append(im)
            re = jnp.concatenate([real[0] - imag[2], real[1]], axis=0)
            im = jnp.concatenate([imag[0] + real[2], imag[1]], axis=0)
            rows.append(jnp.concatenate([re, im], axis=1))
        grid = as_left(jnp.concatenate(rows, axis=0))
        part[s] = lax.dot_general(
            wi[...], grid, (((1,), (1,)), ((), ())), preferred_element_type=F32
        )

        @pl.when(s > 0)
        def _():
            deliver(s - 1)

        return carry

    lax.fori_loop(0, 8, station, 0)
    deliver(7)

    for n in range(8):
        pltpu.make_async_copy(part.at[0], recv.at[n], recv2.at[n]).wait()
    sums = []
    for upper in range(2):
        total = recv[upper]
        for n in range(1, 4):
            total = total + recv[2 * n + upper]
        sums.append(total)
    odd = lanes_of((ROWS, 128)) % 2 == 1
    total = sums[0] + jnp.where(odd, -sums[1], sums[1])
    rows_buf[0:ROWS] = dot(as_left(total), b[...])
    for k in range(NBR):
        for n in range(5):
            real = rows_buf[8 * n:8 * n + 8, 128 * (k // 4):128 * (k // 4) + 128]
            imag = rows_buf[LAGS + 8 * n:LAGS + 8 * n + 8, 256 + 128 * (k // 4):384 + 128 * (k // 4)]
            turn_buf[40 * k + 8 * n:40 * k + 8 * n + 8, :] = pltpu.roll(
                real + imag, (128 - 32 * (k % 4)) % 128, 1
            )
    for n in range(9):
        row = turn_buf[pl.ds(4 * n, 8, stride=40), :]
        for j in range(1, 4 if n < 8 else 1):
            turned = pltpu.roll(turn_buf[pl.ds(4 * n + j, 8, stride=40), :], 32 * j, 1)
            row = jnp.where(lane8 // 32 == j, turned, row)
        if n < 8:
            out[0, :, 128 * n:128 * n + 128] = row
        else:
            out[0, :, 1024:1056] = row[:, :32]

    for copy in sends:
        copy.wait_send()

    @pl.when(gx > 0)
    def _():
        for copy in halo:
            copy.wait_send()

    @pl.when(gx < groups - 1)
    def _():
        for copy in onward:
            copy.wait_send()

    def drain(s, carry):
        @pl.when(jnp.logical_not(jnp.logical_and(y == c, s == 4 * c + ta)))
        def _():
            outgoing(s).wait_send()

        return carry

    lax.fori_loop(0, 8, drain, 0)


def partner_id(gx, y, other, ta):
    return (gx, 2 * y + other, ta)


def solution(mesh):
    groups = mesh.shape["gx"]
    constants = tables()

    def shards(velocity, pressure, offsets):
        any_spec = pl.BlockSpec(memory_space=pltpu.HBM)
        dma = pltpu.SemaphoreType.DMA
        return pl.pallas_call(
            lambda *refs: kernel(groups, *refs),
            out_shape=jax.ShapeDtypeStruct((1, NBR, LAGS * AZIM), F32),
            in_specs=[any_spec, any_spec, pl.BlockSpec(memory_space=pltpu.SMEM)] + [any_spec] * 5,
            out_specs=pl.BlockSpec(memory_space=pltpu.VMEM),
            scratch_shapes=[
                pltpu.VMEM((8, AZIM, 256), F32),
                pltpu.VMEM((32, 16, 256), F32),
                pltpu.VMEM((16, 8, 256), F32),
                pltpu.VMEM((2, 2, 8, 128), F32),
                pltpu.VMEM((2, AZIM, 128), F32),
                *[pltpu.VMEM(table.shape, BF16) for table in constants],
                pltpu.VMEM((8, MODES, 768), F32),
                pltpu.VMEM((24, MODES, 768), F32),
                pltpu.VMEM((8, ROWS, 128), F32),
                pltpu.VMEM((8, ROWS, 128), F32),
                pltpu.VMEM((ROWS + 8, 512), F32),
                pltpu.VMEM((40 * NBR, 128), F32),
                dma((8,)), dma((16,)), dma((3,)), dma((1,)), dma((2,)), dma((2,)),
                dma((2, 4)), dma((8,)), dma((8,)),
            ],
            compiler_params=pltpu.CompilerParams(
                collective_id=0, has_side_effects=True, vmem_limit_bytes=67_000_000
            ),
            name="correlate",
        )(velocity, pressure, offsets, *[jnp.asarray(table) for table in constants])

    return jax.shard_map(
        shards,
        mesh=mesh,
        in_specs=(P("gx", "az", "ta"), P("gx", "az", "ta"), P()),
        out_specs=P(("gx", "az", "ta"), None, None),
        check_vma=False,
    )
```

```python
import math

import jax
import jax.numpy as jnp
import numpy as np
from jax import lax
from jax.experimental import pallas as pl
from jax.experimental.pallas import tpu as pltpu
from jax.sharding import PartitionSpec as P

AZIM = 32
NBR = 8
MAXLAG = 16
LAGS = 33
MODES = 24
LEN = 128
RING = 8
ROWS = 72
MESH = pl.DeviceIdType.MESH
F32, BF16 = jnp.float32, jnp.bfloat16


def halves(table):
    high = table.astype(BF16)
    return high, (table - high.astype(np.float32)).astype(BF16)


def tables():
    mode, azim = np.arange(MODES), np.arange(AZIM)
    angle = 2 * np.pi * ((mode[:, None] * azim[None, :]) % AZIM) / AZIM
    parts = np.stack([np.cos(angle), np.sin(angle)])
    parts[1, 0], parts[1, 16] = 0, 0
    parts[:, 17:] = 0
    eye = np.eye(8)

    def over_stations(part):
        full = np.einsum("st,cmq->csmtq", eye, part)
        return full.reshape(2 * 8 * MODES, 8 * part.shape[2]).astype(np.float32)

    def left(table):
        high, low = halves(table)
        return np.concatenate([high, high, low], axis=1)

    def right(table):
        high, low = halves(table)
        return np.concatenate([high, high, low], axis=0)

    t = np.arange(LEN)
    omega = 2 * np.pi * ((t[:, None] * t[None, :]) % LEN) / LEN
    cos, sin = np.cos(omega), np.sin(omega)
    time = np.block([[cos, -sin], [-sin, -cos]]).astype(np.float32)
    lag = np.arange(-MAXLAG, MAXLAG + 1)
    omega = 2 * np.pi * ((lag[:, None] * t[None, :]) % LEN) / LEN
    cos, sin = np.cos(omega) / LEN, np.sin(omega) / LEN
    back = np.zeros((ROWS, 2 * LEN), np.float32)
    back[: 2 * LAGS] = np.block([[cos, -sin], [sin, cos]])
    slot = np.arange(16)
    angle = 2 * np.pi * ((slot[:, None] * azim[None, :]) % AZIM) / AZIM
    real, imag = 2 * np.cos(angle), -2 * np.sin(angle)
    real[0], imag[0] = 1, np.where(azim % 2 == 0, 1, -1)
    scale = 1.0 / (AZIM * math.sqrt(AZIM * 1024))
    last = np.concatenate([np.kron(eye, real), np.kron(eye, imag)], axis=1) * scale
    return (
        left(over_stations(parts)),
        left(over_stations(parts[:, :, :16])),
        right(time),
        left(back),
        right(last.astype(np.float32)),
    )


def split(value):
    high = value.astype(BF16)
    return high, (value - high.astype(F32)).astype(BF16)


def as_left(value):
    high, low = split(value)
    return jnp.concatenate([high, low, high], axis=1)


def as_right(value):
    high, low = split(value)
    return jnp.concatenate([high, low, high], axis=0)


def dot(left, right):
    return lax.dot_general(left, right, (((1,), (0,)), ((), ())), preferred_element_type=F32)


def lanes_of(shape):
    return lax.broadcasted_iota(jnp.int32, shape, len(shape) - 1)


def kernel(
    groups, vel, pres, t_offs, t_av, t_ap, t_w, t_wi, t_b, out,
    offs, vbuf, pbuf, zbuf, vraw, pack, hal, av, ap, w, wi, b, fv, fp, part, recv, rows_buf, turn_buf,
    local_sem, send_sem, vrecv, precv, zrecv, relay, hrecv, send2, recv2, ring_recv, ready, ring_ready, there,
):
    gx, az, ta = lax.axis_index("gx"), lax.axis_index("az"), lax.axis_index("ta")
    y, c = az // 2, az % 2
    other = 1 - c
    partner = {"gx": gx, "az": 2 * y + other, "ta": ta}
    opens = lax.rem(gx, RING) == 0
    closes = lax.rem(gx, RING) == RING - 1
    ahead_ring = gx < groups - RING
    behind_ring = gx >= RING
    up = jnp.where(opens, gx + RING - 1, gx - 1)
    down = jnp.where(closes, gx - RING + 1, gx + 1)
    has_up = jnp.logical_or(jnp.logical_not(opens), ahead_ring)
    has_down = gx < groups - 1
    lead = jnp.logical_and(gx == 0, az * 4 + ta == 0)
    follows = jnp.logical_and(gx == 0, az * 4 + ta > 0)
    mine = pl.ds(pl.multiple_of(az * 8, 8), 8)
    own_q = pl.ds(pl.multiple_of(c * 8, 8), 8)

    def device(a, t, g=gx):
        return (g, a, t)

    barrier = pltpu.get_barrier_semaphore()
    across = [lax.rem(az + n, 4) for n in range(4)]
    along = [lax.rem(ta + n, 4) for n in range(4)]
    others = [(across[m], along[n]) for m in range(4) for n in (2, 1, 3, 0) if m + n > 0]

    @pl.when(jnp.logical_not(lead))
    def _():
        for a, t in others:
            pl.semaphore_signal(barrier, inc=1, device_id=device(a, t), device_id_type=MESH)

    @pl.when(has_up)
    def _():
        pl.semaphore_signal(barrier, inc=1, device_id=device(az, ta, up), device_id_type=MESH)

    @pl.when(jnp.logical_and(opens, behind_ring))
    def _():
        pl.semaphore_signal(
            barrier, inc=1, device_id=device(az, ta, gx - RING), device_id_type=MESH
        )

    here = [
        pltpu.make_async_copy(vel, vraw, local_sem.at[0]),
        pltpu.make_async_copy(vel.at[pl.ds(8 * c, 8)], vbuf.at[:, mine], local_sem.at[1]),
        pltpu.make_async_copy(pres, pbuf.at[pl.ds(0, 16), own_q], local_sem.at[2]),
    ]
    for number, (source, target) in enumerate(
        [(t_av, av), (t_ap, ap), (t_w, w), (t_wi, wi), (t_b, b), (t_offs, offs)]
    ):
        here.append(pltpu.make_async_copy(source, target, local_sem.at[3 + number]))
    for copy in here:
        copy.start()
    here[0].wait()

    lane8 = lanes_of((8, 128))
    for half in range(2):
        right = jnp.zeros((8, 128), F32)
        left = jnp.zeros((8, 128), F32)
        for j in range(8):
            here_lane = lane8 // 16 == j
            last = vraw[8 * half + j, :, 128:256]
            first = vraw[8 * half + j, :, 0:128]
            right = jnp.where(here_lane, pltpu.roll(last, (16 * j + 16) % 128, 1), right)
            left = jnp.where(here_lane, pltpu.roll(first, 16 * j, 1), left)
        pack[0, half] = right
        pack[1, half] = left

    pl.semaphore_wait(
        barrier,
        15 + has_down.astype(jnp.int32) - follows.astype(jnp.int32)
        + jnp.logical_and(opens, ahead_ring).astype(jnp.int32),
    )

    @pl.when(lead)
    def _():
        for a, t in others:
            pl.semaphore_signal(there, inc=1, device_id=device(a, t), device_id_type=MESH)

    @pl.when(has_down)
    def _():
        pl.semaphore_signal(ready, inc=1, device_id=device(az, ta, down), device_id_type=MESH)

    @pl.when(jnp.logical_and(opens, ahead_ring))
    def _():
        pl.semaphore_signal(
            ring_ready, inc=1, device_id=device(az, ta, gx + RING), device_id_type=MESH
        )

    def remote(source, target, send, receive, to):
        return pltpu.make_async_remote_copy(
            src_ref=source, dst_ref=target, send_sem=send, recv_sem=receive,
            device_id=to, device_id_type=MESH,
        )

    def halo_from(source):
        return [
            remote(
                source.at[pl.ds(8 * n, 8)], pbuf.at[pl.ds(16 + 8 * n, 8), own_q],
                send_sem.at[n], zrecv.at[n], device(az, ta, up),
            )
            for n in range(2)
        ]

    halo, halo_on = halo_from(pres), halo_from(zbuf)
    to_ring = remote(
        pres, zbuf, send_sem.at[16], ring_recv.at[0], device(az, ta, gx - RING)
    )
    hands_on = jnp.logical_and(opens, ahead_ring)
    sends_ring = jnp.logical_and(opens, behind_ring)

    @pl.when(jnp.logical_not(opens))
    def _():
        pl.semaphore_wait(ready, 1)
        for copy in halo:
            copy.start()

    own_half = vel.at[pl.ds(8 * c, 8)]
    other_half = vel.at[pl.ds(8 * other, 8)]
    sends = [
        remote(own_half, vbuf.at[:, mine], send_sem.at[2], vrecv.at[0],
               device(2 * (1 - y) + c, ta)),
        remote(other_half, vbuf.at[:, mine], send_sem.at[3], vrecv.at[1],
               device(2 * (1 - y) + other, ta)),
        remote(other_half, vbuf.at[:, mine], send_sem.at[4], vrecv.at[2],
               device(2 * y + other, ta)),
        remote(pres, pbuf.at[pl.ds(0, 16), own_q], send_sem.at[5], precv.at[0],
               device(2 * y + other, ta)),
    ]
    for a in range(4):
        for side, shift in ((0, 1), (1, 3)):
            sends.append(
                remote(pack.at[side, a % 2], hal.at[side, mine],
                       send_sem.at[6 + 2 * a + side], hrecv.at[side, az],
                       device(a, along[shift]))
            )
    targets = [(2 * (1 - y) + c, ta), (2 * (1 - y) + other, ta)] + [(2 * y + other, ta)] * 2
    targets += [(a, along[shift]) for a in range(4) for shift in (1, 3)]
    to_lead = [jnp.logical_and(gx == 0, a * 4 + t == 0) for a, t in targets]
    for copy, wait_for in zip(sends, to_lead):
        @pl.when(jnp.logical_not(wait_for))
        def _():
            copy.start()

    @pl.when(follows)
    def _():
        pl.semaphore_wait(there, 1)
        for copy, waited_for in zip(sends, to_lead):
            @pl.when(waited_for)
            def _():
                copy.start()

    for copy in here[3:]:
        copy.wait()
    here[2].wait()
    sends[3].wait_recv()

    lane = lanes_of((384, 128))
    zero = jnp.zeros((384, 128), F32)

    def pressure(chunk):
        rows = pbuf[pl.ds(pl.multiple_of(8 * c + 8 * chunk, 8), 8)].reshape(128, 256)
        modes = dot(ap[...], as_right(rows))
        first, second = modes[:, :128], modes[:, 128:]
        windows = [
            jnp.where(lane < 96, first, zero),
            jnp.where(lane < 32, second, jnp.where(lane >= 96, first, zero)),
            jnp.where(lane >= 32, second, zero),
        ]
        for n, window in enumerate(windows):
            both = jnp.concatenate([window[:192], window[192:]], axis=1)
            spectrum = dot(as_left(both), w[...])
            fp[pl.ds(8 * chunk, 8), :, n * 256:(n + 1) * 256] = spectrum.reshape(8, MODES, 256)

    def velocity():
        lane = lanes_of((32, 128))
        low = jnp.where(ta > 0, hal[0], 0.0)
        high = jnp.where(ta < 3, hal[1], 0.0)
        columns = [[], [], []]
        for j in range(8):
            first, second = vbuf[j, :, 0:128], vbuf[j, :, 128:256]
            before = pltpu.roll(low, (112 - 16 * j) % 128, 1)
            after = pltpu.roll(high, (128 - 16 * j) % 128, 1)
            columns[0].append(jnp.where(lane < 112, first, before))
            columns[1].append(jnp.where(lane < 64, second, first))
            columns[2].append(jnp.where(lane >= 16, second, after))
        for n in range(3):
            rows = jnp.concatenate(columns[n], axis=0)
            modes = dot(av[...], as_right(rows))
            both = jnp.concatenate([modes[:192], modes[192:]], axis=1)
            spectrum = dot(as_left(both), w[...])
            fv[:, :, n * 256:(n + 1) * 256] = spectrum.reshape(8, MODES, 256)

    pressure(0)

    @pl.when(sends_ring)
    def _():
        pl.semaphore_wait(ring_ready, 1)
        to_ring.start()

    onward = [
        remote(
            pbuf.at[pl.ds(16 + 8 * n, 8), own_q], pbuf.at[pl.ds(16 + 8 * n, 8), own_q],
            send_sem.at[14 + n], relay.at[n], partner_id(gx, y, other, ta),
        )
        for n in range(2)
    ]

    here[1].wait()
    for copy in sends[:3]:
        copy.wait_recv()
    for side in range(2):
        for a in range(4):
            pltpu.make_async_copy(
                pack.at[0, 0], hal.at[side, pl.ds(8 * a, 8)], hrecv.at[side, a]
            ).wait()
    velocity()

    for n in range(2):
        @pl.when(has_down)
        def _():
            halo[n].wait_recv()
            onward[n].start()
            onward[n].wait_recv()

        @pl.when(jnp.logical_not(has_down))
        def _():
            pbuf[16 + 8 * n:24 + 8 * n] = jnp.zeros((8, 16, 256), F32)

        pressure(1 + n)

    slot = 2 * ta + y

    def target_of(s):
        return device(2 * c + s // 4, s % 4)

    def outgoing(s):
        return remote(part.at[s], recv.at[slot], send2.at[s], recv2.at[slot], target_of(s))

    def deliver(s):
        to_self = jnp.logical_and(y == c, s == 4 * c + ta)

        @pl.when(to_self)
        def _():
            pltpu.make_async_copy(part.at[s], recv.at[slot], recv2.at[slot]).start()

        @pl.when(jnp.logical_not(to_self))
        def _():
            outgoing(s).start()

    def station(s, carry):
        v = [[fv[s, 8 * i:8 * i + 8, 128 * n:128 * n + 128] for n in range(6)] for i in range(3)]
        rows = []
        for k in range(NBR):
            near = s + offs[k]
            real, imag = [], []
            for i in range(3):
                re = im = None
                for n in range(3):
                    vr, vi = v[i][2 * n], v[i][2 * n + 1]
                    pr = fp[near, 8 * i:8 * i + 8, 256 * n:256 * n + 128]
                    pi = fp[near, 8 * i:8 * i + 8, 256 * n + 128:256 * n + 256]
                    one, two = vr * pr + vi * pi, vr * pi - vi * pr
                    re, im = (one, two) if n == 0 else (re + one, im + two)
                real.append(re)
                imag.append(im)
            re = jnp.concatenate([real[0] - imag[2], real[1]], axis=0)
            im = jnp.concatenate([imag[0] + real[2], imag[1]], axis=0)
            rows.append(jnp.concatenate([re, im], axis=1))
        grid = as_left(jnp.concatenate(rows, axis=0))
        part[s] = lax.dot_general(
            wi[...], grid, (((1,), (1,)), ((), ())), preferred_element_type=F32
        )

        @pl.when(s > 0)
        def _():
            deliver(s - 1)

        return carry

    @pl.when(hands_on)
    def _():
        pltpu.make_async_copy(pres, zbuf, ring_recv.at[0]).wait()
        pl.semaphore_wait(ready, 1)
        for copy in halo_on:
            copy.start()

    lax.fori_loop(0, 8, station, 0)
    deliver(7)

    for n in range(8):
        pltpu.make_async_copy(part.at[0], recv.at[n], recv2.at[n]).wait()
    sums = []
    for upper in range(2):
        total = recv[upper]
        for n in range(1, 4):
            total = total + recv[2 * n + upper]
        sums.append(total)
    odd = lanes_of((ROWS, 128)) % 2 == 1
    total = sums[0] + jnp.where(odd, -sums[1], sums[1])
    rows_buf[0:ROWS] = dot(as_left(total), b[...])
    for k in range(NBR):
        for n in range(5):
            real = rows_buf[8 * n:8 * n + 8, 128 * (k // 4):128 * (k // 4) + 128]
            imag = rows_buf[LAGS + 8 * n:LAGS + 8 * n + 8, 256 + 128 * (k // 4):384 + 128 * (k // 4)]
            turn_buf[40 * k + 8 * n:40 * k + 8 * n + 8, :] = pltpu.roll(
                real + imag, (128 - 32 * (k % 4)) % 128, 1
            )
    for n in range(9):
        row = turn_buf[pl.ds(4 * n, 8, stride=40), :]
        for j in range(1, 4 if n < 8 else 1):
            turned = pltpu.roll(turn_buf[pl.ds(4 * n + j, 8, stride=40), :], 32 * j, 1)
            row = jnp.where(lane8 // 32 == j, turned, row)
        if n < 8:
            out[0, :, 128 * n:128 * n + 128] = row
        else:
            out[0, :, 1024:1056] = row[:, :32]

    for copy in sends:
        copy.wait_send()

    @pl.when(has_up)
    def _():
        for copy in halo_on:
            copy.wait_send()

    @pl.when(sends_ring)
    def _():
        to_ring.wait_send()

    @pl.when(has_down)
    def _():
        for copy in onward:
            copy.wait_send()

    def drain(s, carry):
        @pl.when(jnp.logical_not(jnp.logical_and(y == c, s == 4 * c + ta)))
        def _():
            outgoing(s).wait_send()

        return carry

    lax.fori_loop(0, 8, drain, 0)


def partner_id(gx, y, other, ta):
    return (gx, 2 * y + other, ta)


def solution(mesh):
    groups = mesh.shape["gx"]
    constants = tables()

    def shards(velocity, pressure, offsets):
        any_spec = pl.BlockSpec(memory_space=pltpu.HBM)
        dma = pltpu.SemaphoreType.DMA
        return pl.pallas_call(
            lambda *refs: kernel(groups, *refs),
            out_shape=jax.ShapeDtypeStruct((1, NBR, LAGS * AZIM), F32),
            in_specs=[any_spec] * 8,
            out_specs=pl.BlockSpec(memory_space=pltpu.VMEM),
            scratch_shapes=[
                pltpu.SMEM((NBR,), jnp.int32),
                pltpu.VMEM((8, AZIM, 256), F32),
                pltpu.VMEM((32, 16, 256), F32),
                pltpu.VMEM((16, 8, 256), F32),
                pltpu.VMEM((16, 8, 256), F32),
                pltpu.VMEM((2, 2, 8, 128), F32),
                pltpu.VMEM((2, AZIM, 128), F32),
                *[pltpu.VMEM(table.shape, BF16) for table in constants],
                pltpu.VMEM((8, MODES, 768), F32),
                pltpu.VMEM((24, MODES, 768), F32),
                pltpu.VMEM((8, ROWS, 128), F32),
                pltpu.VMEM((8, ROWS, 128), F32),
                pltpu.VMEM((ROWS + 8, 512), F32),
                pltpu.VMEM((40 * NBR, 128), F32),
                dma((9,)), dma((17,)), dma((3,)), dma((1,)), dma((2,)), dma((2,)),
                dma((2, 4)), dma((8,)), dma((8,)),
                dma((1,)), *[pltpu.SemaphoreType.REGULAR] * 3,
            ],
            compiler_params=pltpu.CompilerParams(
                collective_id=0, has_side_effects=True, vmem_limit_bytes=67_000_000
            ),
            name="correlate",
        )(velocity, pressure, offsets, *[jnp.asarray(table) for table in constants])

    return jax.shard_map(
        shards,
        mesh=mesh,
        in_specs=(P("gx", "az", "ta"), P("gx", "az", "ta"), P()),
        out_specs=P(("gx", "az", "ta"), None, None),
        check_vma=False,
    )
```

```python
import math

import jax
import jax.numpy as jnp
import numpy as np
from jax import lax
from jax.experimental import pallas as pl
from jax.experimental.pallas import tpu as pltpu
from jax.sharding import PartitionSpec as P

AZIM = 32
NBR = 8
MAXLAG = 16
LAGS = 33
LEN = 128
HAND_TURN = 3
RING = 8
ROWS = 72
MESH = pl.DeviceIdType.MESH
F32, BF16 = jnp.float32, jnp.bfloat16


def halves(table):
    high = table.astype(BF16)
    return high, (table - high.astype(np.float32)).astype(BF16)


def tables():
    mode, azim = np.arange(17), np.arange(AZIM)
    angle = 2 * np.pi * ((mode[:, None] * azim[None, :]) % AZIM) / AZIM
    parts = np.stack([np.cos(angle), np.sin(angle)])
    parts[1, 0], parts[1, 16] = 0, 0
    eye = np.eye(8)

    def over_stations(part, stations):
        full = np.einsum("st,cmq->csmtq", np.eye(stations), part)
        depth = stations * part.shape[2]
        main = full[:, :, :16].reshape(2 * stations * 16, depth)
        rest = np.zeros((16, depth))
        rest[:stations] = full[0, :, 16].reshape(stations, depth)
        return np.concatenate([main, rest]).astype(np.float32)

    def left(table):
        high, low = halves(table)
        return np.concatenate([high, high, low], axis=1)

    def right(table):
        high, low = halves(table)
        return np.concatenate([high, high, low], axis=0)

    t = np.arange(LEN)
    omega = 2 * np.pi * ((t[:, None] * t[None, :]) % LEN) / LEN
    cos, sin = np.cos(omega), np.sin(omega)
    time = np.block([[cos, -sin], [-sin, -cos]]).astype(np.float32)
    lag = np.arange(-MAXLAG, MAXLAG + 1)
    omega = 2 * np.pi * ((lag[:, None] * t[None, :]) % LEN) / LEN
    cos, sin = np.cos(omega) / LEN, np.sin(omega) / LEN
    back = np.zeros((ROWS, 2 * LEN), np.float32)
    back[: 2 * LAGS] = np.block([[cos, -sin], [sin, cos]])
    slot = np.arange(16)
    angle = 2 * np.pi * ((slot[:, None] * azim[None, :]) % AZIM) / AZIM
    real, imag = 2 * np.cos(angle), -2 * np.sin(angle)
    real[0], imag[0] = 1, np.where(azim % 2 == 0, 1, -1)
    scale = 1.0 / (AZIM * math.sqrt(AZIM * 1024))
    last = np.concatenate([np.kron(eye, real), np.kron(eye, imag)], axis=1) * scale
    return (
        left(over_stations(parts, 4)),
        left(over_stations(parts[:, :, :16], 8)),
        right(time),
        left(back),
        right(last.astype(np.float32)),
    )


def split(value):
    high = value.astype(BF16)
    return high, (value - high.astype(F32)).astype(BF16)


def as_left(value):
    high, low = split(value)
    return jnp.concatenate([high, low, high], axis=1)


def as_right(value):
    high, low = split(value)
    return jnp.concatenate([high, low, high], axis=0)


def dot(left, right):
    return lax.dot_general(left, right, (((1,), (0,)), ((), ())), preferred_element_type=F32)


def lanes_of(shape):
    return lax.broadcasted_iota(jnp.int32, shape, len(shape) - 1)


def kernel(
    groups, vel, pres, t_offs, t_av, t_ap, t_w, t_wi, t_b, out,
    offs, vbuf, pbuf, zbuf, vraw, pack, hal, av, ap, w, wi, b, fv, fp, fv_16, fp_16, part, recv, rows_buf, turn_buf,
    local_sem, send_sem, vrecv, precv, zrecv, relay, hrecv, send2, recv2, ring_recv, ready, ring_ready, there,
):
    gx, az, ta = lax.axis_index("gx"), lax.axis_index("az"), lax.axis_index("ta")
    y, c = az // 2, az % 2
    other = 1 - c
    partner = {"gx": gx, "az": 2 * y + other, "ta": ta}
    opens = lax.rem(gx, RING) == 0
    closes = lax.rem(gx, RING) == RING - 1
    ahead_ring = gx < groups - RING
    behind_ring = gx >= RING
    up = jnp.where(opens, gx + RING - 1, gx - 1)
    down = jnp.where(closes, gx - RING + 1, gx + 1)
    has_up = jnp.logical_or(jnp.logical_not(opens), ahead_ring)
    has_down = gx < groups - 1
    lead = jnp.logical_and(gx == 0, az * 4 + ta == 0)
    follows = jnp.logical_and(gx == 0, az * 4 + ta > 0)
    last_block = gx == groups - 1
    hands_on = jnp.logical_and(opens, ahead_ring)
    sends_ring = jnp.logical_and(opens, behind_ring)
    beside_lead = jnp.logical_and(gx == 0, jnp.logical_and(az == 1, ta == 0))
    halo_to_lead = jnp.logical_and(gx == 1, az * 4 + ta == 0)
    ring_to_lead = jnp.logical_and(gx == RING, az * 4 + ta == 0)
    mine = pl.ds(pl.multiple_of(az * 8, 8), 8)
    own_q = pl.ds(pl.multiple_of(c * 8, 8), 8)

    def device(a, t, g=gx):
        return (g, a, t)

    barrier = pltpu.get_barrier_semaphore()
    across = [lax.rem(az + n, 4) for n in range(4)]
    along = [lax.rem(ta + n, 4) for n in range(4)]
    others = [(across[m], along[n]) for m in range(4) for n in (2, 1, 3, 0) if m + n > 0]

    @pl.when(jnp.logical_not(lead))
    def _():
        for a, t in others:
            pl.semaphore_signal(barrier, inc=1, device_id=device(a, t), device_id_type=MESH)

    def tell(condition, semaphore, block):
        @pl.when(condition)
        def _():
            pl.semaphore_signal(
                semaphore, inc=1, device_id=device(az, ta, block), device_id_type=MESH
            )

    off_lead = jnp.logical_not(lead)
    tell(jnp.logical_and(off_lead, jnp.logical_not(jnp.logical_or(closes, last_block))), barrier, gx + 1)
    tell(jnp.logical_and(off_lead, hands_on), barrier, gx + RING)
    tell(hands_on, barrier, up)
    tell(halo_to_lead, barrier, 0)
    tell(ring_to_lead, barrier, 0)

    here = [
        pltpu.make_async_copy(vel, vraw, local_sem.at[0]),
        pltpu.make_async_copy(vel.at[pl.ds(8 * c, 8)], vbuf.at[:, mine], local_sem.at[1]),
        pltpu.make_async_copy(pres, pbuf.at[pl.ds(0, 16), own_q], local_sem.at[2]),
    ]
    for number, (source, target) in enumerate(
        [(t_av, av), (t_ap, ap), (t_w, w), (t_wi, wi), (t_b, b), (t_offs, offs)]
    ):
        here.append(pltpu.make_async_copy(source, target, local_sem.at[3 + number]))
    for copy in here:
        copy.start()
    here[0].wait()

    lane8 = lanes_of((8, 128))
    for half in range(2):
        right = jnp.zeros((8, 128), F32)
        left = jnp.zeros((8, 128), F32)
        for j in range(8):
            here_lane = lane8 // 16 == j
            last = vraw[8 * half + j, :, 128:256]
            first = vraw[8 * half + j, :, 0:128]
            right = jnp.where(here_lane, pltpu.roll(last, (16 * j + 16) % 128, 1), right)
            left = jnp.where(here_lane, pltpu.roll(first, 16 * j, 1), left)
        pack[0, half] = right
        pack[1, half] = left

    fv_16[...] = jnp.zeros_like(fv_16)
    fp_16[...] = jnp.zeros_like(fp_16)

    counted = [
        jnp.logical_not(jnp.logical_or(opens, halo_to_lead)),
        jnp.logical_and(closes, has_down),
        jnp.logical_and(sends_ring, jnp.logical_not(ring_to_lead)),
        lead, lead,
    ]
    pl.semaphore_wait(
        barrier, 15 - follows.astype(jnp.int32) + sum(one.astype(jnp.int32) for one in counted)
    )

    @pl.when(lead)
    def _():
        for a, t in others:
            pl.semaphore_signal(there, inc=1, device_id=device(a, t), device_id_type=MESH)

    tell(jnp.logical_and(closes, has_down), ready, down)
    tell(lead, ready, 1)
    tell(lead, ring_ready, RING)

    def remote(source, target, send, receive, to):
        return pltpu.make_async_remote_copy(
            src_ref=source, dst_ref=target, send_sem=send, recv_sem=receive,
            device_id=to, device_id_type=MESH,
        )

    def halo_from(source):
        return [
            remote(
                source.at[pl.ds(8 * n, 8)], pbuf.at[pl.ds(16 + 8 * n, 8), own_q],
                send_sem.at[n], zrecv.at[n], device(az, ta, up),
            )
            for n in range(2)
        ]

    halo, halo_on = halo_from(pres), halo_from(zbuf)
    to_ring = [
        remote(
            pres.at[pl.ds(8 * n, 8)], zbuf.at[pl.ds(8 * n, 8)],
            send_sem.at[16 + n], ring_recv.at[n], device(az, ta, gx - RING),
        )
        for n in range(2)
    ]

    @pl.when(jnp.logical_not(jnp.logical_or(opens, halo_to_lead)))
    def _():
        for copy in halo:
            copy.start()

    own_half = vel.at[pl.ds(8 * c, 8)]
    other_half = vel.at[pl.ds(8 * other, 8)]
    sends = [
        remote(own_half, vbuf.at[:, mine], send_sem.at[2], vrecv.at[0],
               device(2 * (1 - y) + c, ta)),
        remote(other_half, vbuf.at[:, mine], send_sem.at[3], vrecv.at[1],
               device(2 * (1 - y) + other, ta)),
        remote(other_half, vbuf.at[:, mine], send_sem.at[4], vrecv.at[2],
               device(2 * y + other, ta)),
        remote(pres, pbuf.at[pl.ds(0, 16), own_q], send_sem.at[5], precv.at[0],
               device(2 * y + other, ta)),
    ]
    for a in range(4):
        for side, shift in ((0, 1), (1, 3)):
            sends.append(
                remote(pack.at[side, a % 2], hal.at[side, mine],
                       send_sem.at[6 + 2 * a + side], hrecv.at[side, az],
                       device(a, along[shift]))
            )
    targets = [(2 * (1 - y) + c, ta), (2 * (1 - y) + other, ta)] + [(2 * y + other, ta)] * 2
    targets += [(a, along[shift]) for a in range(4) for shift in (1, 3)]
    to_lead = [jnp.logical_and(gx == 0, a * 4 + t == 0) for a, t in targets]
    for copy, wait_for in zip(sends, to_lead):
        @pl.when(jnp.logical_not(wait_for))
        def _():
            copy.start()

    @pl.when(jnp.logical_and(sends_ring, jnp.logical_not(ring_to_lead)))
    def _():
        for copy in to_ring:
            copy.start()

    def send_to_lead():
        pl.semaphore_wait(there, 1)
        for copy, waited_for in zip(sends, to_lead):
            @pl.when(waited_for)
            def _():
                copy.start()

    @pl.when(beside_lead)
    def _():
        send_to_lead()

    for copy in here[3:]:
        copy.wait()
    here[2].wait()
    sends[3].wait_recv()

    def spectra(windows, stations, target, target_16, start):
        count = 16 * stations
        parts = []
        for window in windows:
            cosines = jnp.concatenate([window[:count], window[2 * count:2 * count + 8]], axis=0)
            sines = jnp.concatenate([window[count:2 * count], jnp.zeros((8, 128), F32)], axis=0)
            parts.append(jnp.concatenate([cosines, sines], axis=1))
        spectrum = dot(as_left(jnp.concatenate(parts, axis=0)), w[...])
        for n in range(3):
            rows = spectrum[n * (count + 8):(n + 1) * (count + 8)]
            target[start:start + stations, :, n * 256:(n + 1) * 256] = (
                rows[:count].reshape(stations, 16, 256)
            )
            for part_n in range(2):
                first_row = target_16.shape[0] // 6 * (2 * n + part_n) + start
                target_16[first_row:first_row + stations, 0, :] = (
                    rows[count:count + stations, 128 * part_n:128 * part_n + 128]
                )

    def pressure(chunk):
        rows = pbuf[pl.ds(pl.multiple_of(8 * c + 8 * chunk, 8), 8)].reshape(128, 256)
        modes = dot(ap[...], as_right(rows))
        lane = lanes_of((272, 128))
        first, second = modes[:, :128], modes[:, 128:]
        windows = [
            jnp.where(lane < 96, first, 0.0),
            jnp.where(lane < 32, second, jnp.where(lane >= 96, first, 0.0)),
            jnp.where(lane >= 32, second, 0.0),
        ]
        spectra(windows, 8, fp, fp_16, 8 * chunk)

    def velocity():
        lane = lanes_of((32, 128))
        low = jnp.where(ta > 0, hal[0], 0.0)
        high = jnp.where(ta < 3, hal[1], 0.0)
        for half in range(2):
            columns = [[], [], []]
            for j in range(4 * half, 4 * half + 4):
                first, second = vbuf[j, :, 0:128], vbuf[j, :, 128:256]
                before = pltpu.roll(low, (112 - 16 * j) % 128, 1)
                after = pltpu.roll(high, (128 - 16 * j) % 128, 1)
                columns[0].append(jnp.where(lane < 112, first, before))
                columns[1].append(jnp.where(lane < 64, second, first))
                columns[2].append(jnp.where(lane >= 16, second, after))
            rows = jnp.concatenate([jnp.concatenate(col, axis=0) for col in columns], axis=1)
            modes = dot(av[...], as_right(rows))
            spectra([modes[:, 128 * n:128 * n + 128] for n in range(3)], 4, fv, fv_16, 4 * half)

    pressure(0)

    @pl.when(jnp.logical_and(follows, jnp.logical_not(beside_lead)))
    def _():
        send_to_lead()

    @pl.when(halo_to_lead)
    def _():
        pl.semaphore_wait(ready, 1)
        for copy in halo:
            copy.start()

    @pl.when(ring_to_lead)
    def _():
        pl.semaphore_wait(ring_ready, 1)
        for copy in to_ring:
            copy.start()

    onward = [
        remote(
            pbuf.at[pl.ds(16 + 8 * n, 8), own_q], pbuf.at[pl.ds(16 + 8 * n, 8), own_q],
            send_sem.at[14 + n], relay.at[n], partner_id(gx, y, other, ta),
        )
        for n in range(2)
    ]

    for n in range(2):
        @pl.when(has_down)
        def _():
            halo[n].wait_recv()
            onward[n].start()

    here[1].wait()
    for copy in sends[:3]:
        copy.wait_recv()
    for side in range(2):
        for a in range(4):
            pltpu.make_async_copy(
                pack.at[0, 0], hal.at[side, pl.ds(8 * a, 8)], hrecv.at[side, a]
            ).wait()
    velocity()

    for n in range(2):
        @pl.when(has_down)
        def _():
            onward[n].wait_recv()

        @pl.when(jnp.logical_not(has_down))
        def _():
            pbuf[16 + 8 * n:24 + 8 * n] = jnp.zeros((8, 16, 256), F32)

        pressure(1 + n)

    slot = 2 * ta + y

    def station_at(turn):
        ahead = jnp.where(turn < 2, 2, jnp.where(turn < 6, 1 + 2 * (turn % 2), 0))
        core = jnp.where(turn < 2, turn, (turn // 2) % 2)
        core = jnp.where(turn >= 6, turn % 2, core)
        return 4 * core + lax.rem(ta + ahead, 4)

    def target_of(s):
        return device(2 * c + s // 4, s % 4)

    def outgoing(s):
        return remote(part.at[s], recv.at[slot], send2.at[s], recv2.at[slot], target_of(s))

    def deliver(s):
        to_self = jnp.logical_and(y == c, s == 4 * c + ta)

        @pl.when(to_self)
        def _():
            pltpu.make_async_copy(part.at[s], recv.at[slot], recv2.at[slot]).start()

        @pl.when(jnp.logical_not(to_self))
        def _():
            outgoing(s).start()

    def hand_on(n):
        if n == 0:
            pl.semaphore_wait(ready, 1)
        pltpu.make_async_copy(
            pres.at[pl.ds(8 * n, 8)], zbuf.at[pl.ds(8 * n, 8)], ring_recv.at[n]
        ).wait()
        halo_on[n].start()

    @pl.when(hands_on)
    def _():
        hand_on(0)

    def station(turn, carry):
        s = station_at(turn)

        @pl.when(jnp.logical_and(hands_on, turn == HAND_TURN))
        def _():
            hand_on(1)

        v = [
            [fv[s, 0:8, 128 * n:128 * n + 128] for n in range(6)],
            [fv[s, 8:16, 128 * n:128 * n + 128] for n in range(6)],
            [fv_16[8 * n + s] for n in range(6)],
        ]
        rows = []
        for k in range(NBR):
            near = s + offs[k]
            real, imag = [], []
            for i in range(3):
                re = im = None
                for n in range(3):
                    vr, vi = v[i][2 * n], v[i][2 * n + 1]
                    if i < 2:
                        pr = fp[near, 8 * i:8 * i + 8, 256 * n:256 * n + 128]
                        pi = fp[near, 8 * i:8 * i + 8, 256 * n + 128:256 * n + 256]
                    else:
                        pr = fp_16[48 * n + near]
                        pi = fp_16[48 * n + 24 + near]
                    one, two = vr * pr + vi * pi, vr * pi - vi * pr
                    re, im = (one, two) if n == 0 else (re + one, im + two)
                real.append(re)
                imag.append(im)
            re = jnp.concatenate([real[0] - imag[2], real[1]], axis=0)
            im = jnp.concatenate([imag[0] + real[2], imag[1]], axis=0)
            rows.append(jnp.concatenate([re, im], axis=1))
        grid = as_left(jnp.concatenate(rows, axis=0))
        part[s] = lax.dot_general(
            wi[...], grid, (((1,), (1,)), ((), ())), preferred_element_type=F32
        )

        @pl.when(turn > 0)
        def _():
            deliver(station_at(turn - 1))

        return carry

    lax.fori_loop(0, 8, station, 0)
    deliver(station_at(7))

    for n in range(8):
        pltpu.make_async_copy(part.at[0], recv.at[n], recv2.at[n]).wait()
    sums = []
    for upper in range(2):
        total = recv[upper]
        for n in range(1, 4):
            total = total + recv[2 * n + upper]
        sums.append(total)
    odd = lanes_of((ROWS, 128)) % 2 == 1
    total = sums[0] + jnp.where(odd, -sums[1], sums[1])
    rows_buf[0:ROWS] = dot(as_left(total), b[...])
    for k in range(NBR):
        for n in range(5):
            real = rows_buf[8 * n:8 * n + 8, 128 * (k // 4):128 * (k // 4) + 128]
            imag = rows_buf[LAGS + 8 * n:LAGS + 8 * n + 8, 256 + 128 * (k // 4):384 + 128 * (k // 4)]
            turn_buf[40 * k + 8 * n:40 * k + 8 * n + 8, :] = pltpu.roll(
                real + imag, (128 - 32 * (k % 4)) % 128, 1
            )
    for n in range(9):
        row = turn_buf[pl.ds(4 * n, 8, stride=40), :]
        for j in range(1, 4 if n < 8 else 1):
            turned = pltpu.roll(turn_buf[pl.ds(4 * n + j, 8, stride=40), :], 32 * j, 1)
            row = jnp.where(lane8 // 32 == j, turned, row)
        if n < 8:
            out[0, :, 128 * n:128 * n + 128] = row
        else:
            out[0, :, 1024:1056] = row[:, :32]

    for copy in sends:
        copy.wait_send()

    @pl.when(has_up)
    def _():
        for copy in halo_on:
            copy.wait_send()

    @pl.when(sends_ring)
    def _():
        for copy in to_ring:
            copy.wait_send()

    @pl.when(has_down)
    def _():
        for copy in onward:
            copy.wait_send()

    def drain(s, carry):
        @pl.when(jnp.logical_not(jnp.logical_and(y == c, s == 4 * c + ta)))
        def _():
            outgoing(s).wait_send()

        return carry

    lax.fori_loop(0, 8, drain, 0)


def partner_id(gx, y, other, ta):
    return (gx, 2 * y + other, ta)


def solution(mesh):
    groups = mesh.shape["gx"]
    constants = tables()

    def shards(velocity, pressure, offsets):
        any_spec = pl.BlockSpec(memory_space=pltpu.HBM)
        dma = pltpu.SemaphoreType.DMA
        return pl.pallas_call(
            lambda *refs: kernel(groups, *refs),
            out_shape=jax.ShapeDtypeStruct((1, NBR, LAGS * AZIM), F32),
            in_specs=[any_spec] * 8,
            out_specs=pl.BlockSpec(memory_space=pltpu.VMEM),
            scratch_shapes=[
                pltpu.SMEM((NBR,), jnp.int32),
                pltpu.VMEM((8, AZIM, 256), F32),
                pltpu.VMEM((32, 16, 256), F32),
                pltpu.VMEM((16, 8, 256), F32),
                pltpu.VMEM((16, 8, 256), F32),
                pltpu.VMEM((2, 2, 8, 128), F32),
                pltpu.VMEM((2, AZIM, 128), F32),
                *[pltpu.VMEM(table.shape, BF16) for table in constants],
                pltpu.VMEM((8, 16, 768), F32),
                pltpu.VMEM((24, 16, 768), F32),
                pltpu.VMEM((48, 8, 128), F32),
                pltpu.VMEM((144, 8, 128), F32),
                pltpu.VMEM((8, ROWS, 128), F32),
                pltpu.VMEM((8, ROWS, 128), F32),
                pltpu.VMEM((ROWS + 8, 512), F32),
                pltpu.VMEM((40 * NBR, 128), F32),
                dma((9,)), dma((18,)), dma((3,)), dma((1,)), dma((2,)), dma((2,)),
                dma((2, 4)), dma((8,)), dma((8,)),
                dma((2,)), *[pltpu.SemaphoreType.REGULAR] * 3,
            ],
            compiler_params=pltpu.CompilerParams(
                collective_id=0, has_side_effects=True, vmem_limit_bytes=67_000_000
            ),
            name="correlate",
        )(velocity, pressure, offsets, *[jnp.asarray(table) for table in constants])

    return jax.shard_map(
        shards,
        mesh=mesh,
        in_specs=(P("gx", "az", "ta"), P("gx", "az", "ta"), P()),
        out_specs=P(("gx", "az", "ta"), None, None),
        check_vma=False,
    )
```

```python
import math

import jax
import jax.numpy as jnp
import numpy as np
from jax import lax
from jax.experimental import pallas as pl
from jax.experimental.pallas import tpu as pltpu
from jax.sharding import PartitionSpec as P

AZIM = 32
NBR = 8
MAXLAG = 16
LAGS = 33
LEN = 128
RING = 8
ROWS = 72
MESH = pl.DeviceIdType.MESH
F32, BF16 = jnp.float32, jnp.bfloat16


def halves(table):
    high = table.astype(BF16)
    return high, (table - high.astype(np.float32)).astype(BF16)


def tables():
    mode, azim = np.arange(17), np.arange(AZIM)
    angle = 2 * np.pi * ((mode[:, None] * azim[None, :]) % AZIM) / AZIM
    parts = np.stack([np.cos(angle), np.sin(angle)])
    parts[1, 0], parts[1, 16] = 0, 0
    eye = np.eye(8)

    def over_stations(part, stations):
        full = np.einsum("st,cmq->csmtq", np.eye(stations), part)
        depth = stations * part.shape[2]
        main = full[:, :, :16].reshape(2 * stations * 16, depth)
        rest = np.zeros((16, depth))
        rest[:stations] = full[0, :, 16].reshape(stations, depth)
        return np.concatenate([main, rest]).astype(np.float32)

    def left(table):
        high, low = halves(table)
        return np.concatenate([high, high, low], axis=1)

    def right(table):
        high, low = halves(table)
        return np.concatenate([high, high, low], axis=0)

    t = np.arange(LEN)
    omega = 2 * np.pi * ((t[:, None] * t[None, :]) % LEN) / LEN
    cos, sin = np.cos(omega), np.sin(omega)
    time = np.block([[cos, -sin], [-sin, -cos]]).astype(np.float32)
    lag = np.arange(-MAXLAG, MAXLAG + 1)
    omega = 2 * np.pi * ((lag[:, None] * t[None, :]) % LEN) / LEN
    cos, sin = np.cos(omega) / LEN, np.sin(omega) / LEN
    back = np.zeros((ROWS, 2 * LEN), np.float32)
    back[: 2 * LAGS] = np.block([[cos, -sin], [sin, cos]])
    slot = np.arange(16)
    angle = 2 * np.pi * ((slot[:, None] * azim[None, :]) % AZIM) / AZIM
    real, imag = 2 * np.cos(angle), -2 * np.sin(angle)
    real[0], imag[0] = 1, np.where(azim % 2 == 0, 1, -1)
    scale = 1.0 / (AZIM * math.sqrt(AZIM * 1024))
    last = np.concatenate([np.kron(eye, real), np.kron(eye, imag)], axis=1) * scale
    return (
        left(over_stations(parts, 4)),
        left(over_stations(parts[:, :, :16], 8)),
        right(time),
        left(back),
        right(last.astype(np.float32)),
    )


def split(value):
    high = value.astype(BF16)
    return high, (value - high.astype(F32)).astype(BF16)


def as_left(value):
    high, low = split(value)
    return jnp.concatenate([high, low, high], axis=1)


def as_right(value):
    high, low = split(value)
    return jnp.concatenate([high, low, high], axis=0)


def dot(left, right):
    return lax.dot_general(left, right, (((1,), (0,)), ((), ())), preferred_element_type=F32)


def lanes_of(shape):
    return lax.broadcasted_iota(jnp.int32, shape, len(shape) - 1)


def kernel(
    groups, vel, pres, t_offs, t_av, t_ap, t_w, t_wi, t_b, out,
    offs, vbuf, pbuf, zbuf, vraw, pack, hal, av, ap, w, wi, b, fv, fp, fv_16, fp_16, part, recv, rows_buf, turn_buf,
    local_sem, send_sem, vrecv, precv, zrecv, relay, hrecv, send2, recv2, ring_recv, ready, there,
):
    gx, az, ta = lax.axis_index("gx"), lax.axis_index("az"), lax.axis_index("ta")
    y, c = az // 2, az % 2
    other = 1 - c
    partner = {"gx": gx, "az": 2 * y + other, "ta": ta}
    opens = lax.rem(gx, RING) == 0
    closes = lax.rem(gx, RING) == RING - 1
    ahead_ring = gx < groups - RING
    behind_ring = gx >= RING
    up = jnp.where(opens, gx + RING - 1, gx - 1)
    down = jnp.where(closes, gx - RING + 1, gx + 1)
    has_down = gx < groups - 1
    lead = jnp.logical_and(gx == 0, az * 4 + ta == 0)
    follows = jnp.logical_and(gx == 0, az * 4 + ta > 0)
    last_block = gx == groups - 1
    hands_on = jnp.logical_and(jnp.logical_and(opens, ahead_ring), y == 1)
    sends_ring = jnp.logical_and(opens, behind_ring)
    beside_lead = jnp.logical_and(gx == 0, jnp.logical_and(az == 1, ta == 0))
    halo_to_lead = jnp.logical_and(gx == 1, az * 4 + ta == 0)
    mine = pl.ds(pl.multiple_of(az * 8, 8), 8)
    own_q = pl.ds(pl.multiple_of(c * 8, 8), 8)

    def device(a, t, g=gx):
        return (g, a, t)

    barrier = pltpu.get_barrier_semaphore()
    across = [lax.rem(az + n, 4) for n in range(4)]
    along = [lax.rem(ta + n, 4) for n in range(4)]
    others = [(across[m], along[n]) for m in range(4) for n in (2, 1, 3, 0) if m + n > 0]

    @pl.when(jnp.logical_not(lead))
    def _():
        for a, t in others:
            pl.semaphore_signal(barrier, inc=1, device_id=device(a, t), device_id_type=MESH)

    def tell(condition, semaphore, block, row=az):
        @pl.when(condition)
        def _():
            pl.semaphore_signal(
                semaphore, inc=1, device_id=device(row, ta, block), device_id_type=MESH
            )

    off_lead = jnp.logical_not(lead)
    second = c == 1
    told = jnp.logical_not(jnp.logical_or(closes, last_block))
    tell(jnp.logical_and(off_lead, told), barrier, gx + 1)
    tell(jnp.logical_and(second, told), barrier, gx + 1, 2 * y)
    for upper in range(2):
        tell(hands_on, barrier, gx + RING, 2 * upper + c)
        tell(hands_on, barrier, up, 2 * upper + c)
        tell(jnp.logical_and(hands_on, c == 0), barrier, up, 2 * upper + 1)
    tell(halo_to_lead, barrier, 0)

    here = [
        pltpu.make_async_copy(vel, vraw, local_sem.at[0]),
        pltpu.make_async_copy(vel.at[pl.ds(8 * c, 8)], vbuf.at[:, mine], local_sem.at[1]),
        pltpu.make_async_copy(pres, pbuf.at[pl.ds(0, 16), own_q], local_sem.at[2]),
    ]
    for number, (source, target) in enumerate(
        [(t_av, av), (t_ap, ap), (t_w, w), (t_wi, wi), (t_b, b), (t_offs, offs)]
    ):
        here.append(pltpu.make_async_copy(source, target, local_sem.at[3 + number]))
    for copy in here:
        copy.start()
    here[0].wait()

    lane8 = lanes_of((8, 128))
    for half in range(2):
        right = jnp.zeros((8, 128), F32)
        left = jnp.zeros((8, 128), F32)
        for j in range(8):
            here_lane = lane8 // 16 == j
            last = vraw[8 * half + j, :, 128:256]
            first = vraw[8 * half + j, :, 0:128]
            right = jnp.where(here_lane, pltpu.roll(last, (16 * j + 16) % 128, 1), right)
            left = jnp.where(here_lane, pltpu.roll(first, 16 * j, 1), left)
        pack[0, half] = right
        pack[1, half] = left

    fv_16[...] = jnp.zeros_like(fv_16)
    fp_16[...] = jnp.zeros_like(fp_16)

    counted = [
        jnp.logical_not(jnp.logical_or(opens, halo_to_lead)),
        jnp.logical_and(jnp.logical_not(opens), c == 0),
        jnp.logical_and(closes, has_down),
        jnp.logical_and(jnp.logical_and(closes, has_down), second),
        sends_ring,
        lead,
    ]
    pl.semaphore_wait(
        barrier, 15 - follows.astype(jnp.int32) + sum(one.astype(jnp.int32) for one in counted)
    )

    @pl.when(lead)
    def _():
        for a, t in others:
            pl.semaphore_signal(there, inc=1, device_id=device(a, t), device_id_type=MESH)

    tell(jnp.logical_and(closes, has_down), ready, down, 2 + c)
    tell(jnp.logical_and(jnp.logical_and(closes, has_down), second), ready, down, 2)
    tell(lead, ready, 1)

    def remote(source, target, send, receive, to):
        return pltpu.make_async_remote_copy(
            src_ref=source, dst_ref=target, send_sem=send, recv_sem=receive,
            device_id=to, device_id_type=MESH,
        )

    def halo_from(source, row, sems):
        return [
            remote(
                source.at[pl.ds(8 * n, 8)], pbuf.at[pl.ds(16 + 8 * n, 8), own_q],
                send_sem.at[sems + n], zrecv.at[n * (1 + c)], device(row + n * (1 - c), ta, up),
            )
            for n in range(2)
        ]

    halo = halo_from(pres, az, 0)
    halo_on = [halo_from(zbuf.at[upper], 2 * upper + c, 18 * (1 - upper)) for upper in range(2)]
    to_ring = [
        remote(
            pres.at[pl.ds(8 * n, 8)], zbuf.at[y, pl.ds(8 * n, 8)],
            send_sem.at[16 + n], ring_recv.at[y, n], device(2 + c, ta, gx - RING),
        )
        for n in range(2)
    ]

    own_half = vel.at[pl.ds(8 * c, 8)]
    other_half = vel.at[pl.ds(8 * other, 8)]
    sends = [
        remote(own_half, vbuf.at[:, mine], send_sem.at[2], vrecv.at[0],
               device(2 * (1 - y) + c, ta)),
        remote(other_half, vbuf.at[:, mine], send_sem.at[3], vrecv.at[1],
               device(2 * (1 - y) + other, ta)),
        remote(other_half, vbuf.at[:, mine], send_sem.at[4], vrecv.at[2],
               device(2 * y + other, ta)),
        remote(pres, pbuf.at[pl.ds(0, 16), own_q], send_sem.at[5], precv.at[0],
               device(2 * y + other, ta)),
    ]
    for a in range(4):
        for side, shift in ((0, 1), (1, 3)):
            sends.append(
                remote(pack.at[side, a % 2], hal.at[side, mine],
                       send_sem.at[6 + 2 * a + side], hrecv.at[side, az],
                       device(a, along[shift]))
            )
    targets = [(2 * (1 - y) + c, ta), (2 * (1 - y) + other, ta)] + [(2 * y + other, ta)] * 2
    targets += [(a, along[shift]) for a in range(4) for shift in (1, 3)]
    to_lead = [jnp.logical_and(gx == 0, a * 4 + t == 0) for a, t in targets]
    def start(numbers):
        for n in numbers:
            @pl.when(jnp.logical_not(to_lead[n]))
            def _():
                sends[n].start()

    start(range(4, 12))
    start((0, 1))

    @pl.when(jnp.logical_not(jnp.logical_or(opens, halo_to_lead)))
    def _():
        for copy in halo:
            copy.start()

    start((3, 2))

    @pl.when(sends_ring)
    def _():
        for copy in to_ring:
            copy.start()

    def send_to_lead():
        pl.semaphore_wait(there, 1)
        for copy, waited_for in zip(sends, to_lead):
            @pl.when(waited_for)
            def _():
                copy.start()

    @pl.when(beside_lead)
    def _():
        send_to_lead()

    for copy in here[3:]:
        copy.wait()
    here[2].wait()
    sends[3].wait_recv()

    def spectra(windows, stations, target, target_16, start):
        count = 16 * stations
        parts = []
        for window in windows:
            cosines = jnp.concatenate([window[:count], window[2 * count:2 * count + 8]], axis=0)
            sines = jnp.concatenate([window[count:2 * count], jnp.zeros((8, 128), F32)], axis=0)
            parts.append(jnp.concatenate([cosines, sines], axis=1))
        spectrum = dot(as_left(jnp.concatenate(parts, axis=0)), w[...])
        for n in range(3):
            rows = spectrum[n * (count + 8):(n + 1) * (count + 8)]
            target[start:start + stations, :, n * 256:(n + 1) * 256] = (
                rows[:count].reshape(stations, 16, 256)
            )
            for part_n in range(2):
                first_row = target_16.shape[0] // 6 * (2 * n + part_n) + start
                target_16[first_row:first_row + stations, 0, :] = (
                    rows[count:count + stations, 128 * part_n:128 * part_n + 128]
                )

    def pressure(chunk):
        rows = pbuf[pl.ds(pl.multiple_of(8 * c + 8 * chunk, 8), 8)].reshape(128, 256)
        modes = dot(ap[...], as_right(rows))
        lane = lanes_of((272, 128))
        first, second = modes[:, :128], modes[:, 128:]
        windows = [
            jnp.where(lane < 96, first, 0.0),
            jnp.where(lane < 32, second, jnp.where(lane >= 96, first, 0.0)),
            jnp.where(lane >= 32, second, 0.0),
        ]
        spectra(windows, 8, fp, fp_16, 8 * chunk)

    def velocity():
        lane = lanes_of((32, 128))
        low = jnp.where(ta > 0, hal[0], 0.0)
        high = jnp.where(ta < 3, hal[1], 0.0)
        for half in range(2):
            columns = [[], [], []]
            for j in range(4 * half, 4 * half + 4):
                first, second = vbuf[j, :, 0:128], vbuf[j, :, 128:256]
                before = pltpu.roll(low, (112 - 16 * j) % 128, 1)
                after = pltpu.roll(high, (128 - 16 * j) % 128, 1)
                columns[0].append(jnp.where(lane < 112, first, before))
                columns[1].append(jnp.where(lane < 64, second, first))
                columns[2].append(jnp.where(lane >= 16, second, after))
            rows = jnp.concatenate([jnp.concatenate(col, axis=0) for col in columns], axis=1)
            modes = dot(av[...], as_right(rows))
            spectra([modes[:, 128 * n:128 * n + 128] for n in range(3)], 4, fv, fv_16, 4 * half)

    pressure(0)

    @pl.when(jnp.logical_and(follows, jnp.logical_not(beside_lead)))
    def _():
        send_to_lead()

    @pl.when(halo_to_lead)
    def _():
        pl.semaphore_wait(ready, 1)
        for copy in halo:
            copy.start()

    onward = remote(
        pbuf.at[pl.ds(16, 8), own_q], pbuf.at[pl.ds(16, 8), own_q],
        send_sem.at[14], relay.at[0], partner_id(gx, y, other, ta),
    )

    def arrived(n):
        pltpu.make_async_copy(
            pres.at[pl.ds(0, 8)], pbuf.at[pl.ds(16, 8), own_q], zrecv.at[n]
        ).wait()

    @pl.when(has_down)
    def _():
        arrived(0)
        onward.start()

    @pl.when(jnp.logical_not(has_down))
    def _():
        pbuf[16:32] = jnp.zeros((16, 16, 256), F32)

    @pl.when(jnp.logical_and(has_down, second))
    def _():
        onward.wait_recv()

    pressure(1)
    here[1].wait()
    for copy in sends[:3]:
        copy.wait_recv()
    for side in range(2):
        for a in range(4):
            pltpu.make_async_copy(
                pack.at[0, 0], hal.at[side, pl.ds(8 * a, 8)], hrecv.at[side, a]
            ).wait()
    velocity()

    @pl.when(jnp.logical_and(has_down, c == 0))
    def _():
        onward.wait_recv()

    @pl.when(jnp.logical_and(has_down, second))
    def _():
        arrived(1)
        arrived(2)

    pressure(2)

    slot = 2 * ta + y

    def station_at(turn):
        ahead = jnp.where(turn < 2, 2, jnp.where(turn < 6, 1 + 2 * (turn % 2), 0))
        core = jnp.where(turn < 2, turn, (turn // 2) % 2)
        core = jnp.where(turn >= 6, turn % 2, core)
        return 4 * core + lax.rem(ta + ahead, 4)

    def target_of(s):
        return device(2 * c + s // 4, s % 4)

    def outgoing(s):
        return remote(part.at[s], recv.at[slot], send2.at[s], recv2.at[slot], target_of(s))

    def deliver(s):
        to_self = jnp.logical_and(y == c, s == 4 * c + ta)

        @pl.when(to_self)
        def _():
            pltpu.make_async_copy(part.at[s], recv.at[slot], recv2.at[slot]).start()

        @pl.when(jnp.logical_not(to_self))
        def _():
            outgoing(s).start()

    def hand_on(n):
        if n == 0:
            pl.semaphore_wait(ready, 4 - 2 * c)
        for upper in (1, 0):
            pltpu.make_async_copy(
                pres.at[pl.ds(8 * n, 8)], zbuf.at[upper, pl.ds(8 * n, 8)], ring_recv.at[upper, n]
            ).wait()
            halo_on[upper][n].start()

    def station(turn, carry):
        s = station_at(turn)

        for n in range(2):
            @pl.when(jnp.logical_and(hands_on, turn == 3 * n + 2 * (gx == 0).astype(jnp.int32)))
            def _():
                hand_on(n)

        v = [
            [fv[s, 0:8, 128 * n:128 * n + 128] for n in range(6)],
            [fv[s, 8:16, 128 * n:128 * n + 128] for n in range(6)],
            [fv_16[8 * n + s] for n in range(6)],
        ]
        rows = []
        for k in range(NBR):
            near = s + offs[k]
            real, imag = [], []
            for i in range(3):
                re = im = None
                for n in range(3):
                    vr, vi = v[i][2 * n], v[i][2 * n + 1]
                    if i < 2:
                        pr = fp[near, 8 * i:8 * i + 8, 256 * n:256 * n + 128]
                        pi = fp[near, 8 * i:8 * i + 8, 256 * n + 128:256 * n + 256]
                    else:
                        pr = fp_16[48 * n + near]
                        pi = fp_16[48 * n + 24 + near]
                    one, two = vr * pr + vi * pi, vr * pi - vi * pr
                    re, im = (one, two) if n == 0 else (re + one, im + two)
                real.append(re)
                imag.append(im)
            re = jnp.concatenate([real[0] - imag[2], real[1]], axis=0)
            im = jnp.concatenate([imag[0] + real[2], imag[1]], axis=0)
            rows.append(jnp.concatenate([re, im], axis=1))
        grid = as_left(jnp.concatenate(rows, axis=0))
        part[s] = lax.dot_general(
            wi[...], grid, (((1,), (1,)), ((), ())), preferred_element_type=F32
        )

        @pl.when(turn > 0)
        def _():
            deliver(station_at(turn - 1))

        return carry

    lax.fori_loop(0, 8, station, 0)
    deliver(station_at(7))

    for n in range(8):
        pltpu.make_async_copy(part.at[0], recv.at[n], recv2.at[n]).wait()
    sums = []
    for upper in range(2):
        total = recv[upper]
        for n in range(1, 4):
            total = total + recv[2 * n + upper]
        sums.append(total)
    odd = lanes_of((ROWS, 128)) % 2 == 1
    total = sums[0] + jnp.where(odd, -sums[1], sums[1])
    rows_buf[0:ROWS] = dot(as_left(total), b[...])
    for k in range(NBR):
        for n in range(5):
            real = rows_buf[8 * n:8 * n + 8, 128 * (k // 4):128 * (k // 4) + 128]
            imag = rows_buf[LAGS + 8 * n:LAGS + 8 * n + 8, 256 + 128 * (k // 4):384 + 128 * (k // 4)]
            turn_buf[40 * k + 8 * n:40 * k + 8 * n + 8, :] = pltpu.roll(
                real + imag, (128 - 32 * (k % 4)) % 128, 1
            )
    for n in range(9):
        row = turn_buf[pl.ds(4 * n, 8, stride=40), :]
        for j in range(1, 4 if n < 8 else 1):
            turned = pltpu.roll(turn_buf[pl.ds(4 * n + j, 8, stride=40), :], 32 * j, 1)
            row = jnp.where(lane8 // 32 == j, turned, row)
        if n < 8:
            out[0, :, 128 * n:128 * n + 128] = row
        else:
            out[0, :, 1024:1056] = row[:, :32]

    for copy in sends:
        copy.wait_send()

    @pl.when(jnp.logical_not(opens))
    def _():
        for copy in halo:
            copy.wait_send()

    @pl.when(hands_on)
    def _():
        for copy in halo_on[0] + halo_on[1]:
            copy.wait_send()

    @pl.when(sends_ring)
    def _():
        for copy in to_ring:
            copy.wait_send()

    @pl.when(has_down)
    def _():
        onward.wait_send()

    def drain(s, carry):
        @pl.when(jnp.logical_not(jnp.logical_and(y == c, s == 4 * c + ta)))
        def _():
            outgoing(s).wait_send()

        return carry

    lax.fori_loop(0, 8, drain, 0)


def partner_id(gx, y, other, ta):
    return (gx, 2 * y + other, ta)


def solution(mesh):
    groups = mesh.shape["gx"]
    constants = tables()

    def shards(velocity, pressure, offsets):
        any_spec = pl.BlockSpec(memory_space=pltpu.HBM)
        dma = pltpu.SemaphoreType.DMA
        return pl.pallas_call(
            lambda *refs: kernel(groups, *refs),
            out_shape=jax.ShapeDtypeStruct((1, NBR, LAGS * AZIM), F32),
            in_specs=[any_spec] * 8,
            out_specs=pl.BlockSpec(memory_space=pltpu.VMEM),
            scratch_shapes=[
                pltpu.SMEM((NBR,), jnp.int32),
                pltpu.VMEM((8, AZIM, 256), F32),
                pltpu.VMEM((32, 16, 256), F32),
                pltpu.VMEM((2, 16, 8, 256), F32),
                pltpu.VMEM((16, 8, 256), F32),
                pltpu.VMEM((2, 2, 8, 128), F32),
                pltpu.VMEM((2, AZIM, 128), F32),
                *[pltpu.VMEM(table.shape, BF16) for table in constants],
                pltpu.VMEM((8, 16, 768), F32),
                pltpu.VMEM((24, 16, 768), F32),
                pltpu.VMEM((48, 8, 128), F32),
                pltpu.VMEM((144, 8, 128), F32),
                pltpu.VMEM((8, ROWS, 128), F32),
                pltpu.VMEM((8, ROWS, 128), F32),
                pltpu.VMEM((ROWS + 8, 512), F32),
                pltpu.VMEM((40 * NBR, 128), F32),
                dma((9,)), dma((20,)), dma((3,)), dma((1,)), dma((3,)), dma((1,)),
                dma((2, 4)), dma((8,)), dma((8,)),
                dma((2, 2)), *[pltpu.SemaphoreType.REGULAR] * 2,
            ],
            compiler_params=pltpu.CompilerParams(
                collective_id=0, has_side_effects=True, vmem_limit_bytes=67_000_000
            ),
            name="correlate",
        )(velocity, pressure, offsets, *[jnp.asarray(table) for table in constants])

    return jax.shard_map(
        shards,
        mesh=mesh,
        in_specs=(P("gx", "az", "ta"), P("gx", "az", "ta"), P()),
        out_specs=P(("gx", "az", "ta"), None, None),
        check_vma=False,
    )
```

```python
import math

import jax
import jax.numpy as jnp
import numpy as np
from jax import lax
from jax.experimental import pallas as pl
from jax.experimental.pallas import tpu as pltpu
from jax.sharding import PartitionSpec as P

AZIM = 32
NBR = 8
MAXLAG = 16
LAGS = 33
LEN = 128
RING = 8
HAND_PAIRS = ((2, 0), (4, 4))
ROWS = 72
MESH = pl.DeviceIdType.MESH
F32, BF16 = jnp.float32, jnp.bfloat16


def halves(table):
    high = table.astype(BF16)
    return high, (table - high.astype(np.float32)).astype(BF16)


def tables():
    mode, azim = np.arange(17), np.arange(AZIM)
    angle = 2 * np.pi * ((mode[:, None] * azim[None, :]) % AZIM) / AZIM
    parts = np.stack([np.cos(angle), np.sin(angle)])
    parts[1, 0], parts[1, 16] = 0, 0
    eye = np.eye(8)

    def over_stations(part, stations):
        full = np.einsum("st,cmq->csmtq", np.eye(stations), part)
        depth = stations * part.shape[2]
        main = full[:, :, :16].reshape(2 * stations * 16, depth)
        rest = np.zeros((16, depth))
        rest[:stations] = full[0, :, 16].reshape(stations, depth)
        return np.concatenate([main, rest]).astype(np.float32)

    def left(table):
        high, low = halves(table)
        return np.concatenate([high, high, low], axis=1)

    def right(table):
        high, low = halves(table)
        return np.concatenate([high, high, low], axis=0)

    t = np.arange(LEN)
    omega = 2 * np.pi * ((t[:, None] * t[None, :]) % LEN) / LEN
    cos, sin = np.cos(omega), np.sin(omega)
    time = np.block([[cos, -sin], [-sin, -cos]]).astype(np.float32)
    lag = np.arange(-MAXLAG, MAXLAG + 1)
    omega = 2 * np.pi * ((lag[:, None] * t[None, :]) % LEN) / LEN
    cos, sin = np.cos(omega) / LEN, np.sin(omega) / LEN
    back = np.zeros((ROWS, 2 * LEN), np.float32)
    back[: 2 * LAGS] = np.block([[cos, -sin], [sin, cos]])
    slot = np.arange(16)
    angle = 2 * np.pi * ((slot[:, None] * azim[None, :]) % AZIM) / AZIM
    real, imag = 2 * np.cos(angle), -2 * np.sin(angle)
    real[0], imag[0] = 1, np.where(azim % 2 == 0, 1, -1)
    scale = 1.0 / (AZIM * math.sqrt(AZIM * 1024))
    last = np.concatenate([np.kron(eye, real), np.kron(eye, imag)], axis=1) * scale
    return (
        left(over_stations(parts, 4)),
        left(over_stations(parts[:, :, :16], 8)),
        right(time),
        left(back),
        right(last.astype(np.float32)),
    )


def split(value):
    high = value.astype(BF16)
    return high, (value - high.astype(F32)).astype(BF16)


def as_left(value):
    high, low = split(value)
    return jnp.concatenate([high, low, high], axis=1)


def as_right(value):
    high, low = split(value)
    return jnp.concatenate([high, low, high], axis=0)


def dot(left, right):
    return lax.dot_general(left, right, (((1,), (0,)), ((), ())), preferred_element_type=F32)


def lanes_of(shape):
    return lax.broadcasted_iota(jnp.int32, shape, len(shape) - 1)


def kernel(
    groups, vel, pres, t_offs, t_av, t_ap, t_w, t_wi, t_b, out,
    offs, vbuf, pbuf, zbuf, vraw, pack, hal, av, ap, w, wi, b, fv, fp, fv_16, fp_16, part, recv, rows_buf, turn_buf,
    local_sem, send_sem, vrecv, precv, zrecv, relay, hrecv, send2, recv2, ring_recv, ready, there,
):
    gx, az, ta = lax.axis_index("gx"), lax.axis_index("az"), lax.axis_index("ta")
    y, c = az // 2, az % 2
    other = 1 - c
    partner = {"gx": gx, "az": 2 * y + other, "ta": ta}
    opens = lax.rem(gx, RING) == 0
    closes = lax.rem(gx, RING) == RING - 1
    ahead_ring = gx < groups - RING
    behind_ring = gx >= RING
    up = jnp.where(opens, gx + RING - 1, gx - 1)
    down = jnp.where(closes, gx - RING + 1, gx + 1)
    has_down = gx < groups - 1
    lead = jnp.logical_and(gx == 0, az * 4 + ta == 0)
    follows = jnp.logical_and(gx == 0, az * 4 + ta > 0)
    last_block = gx == groups - 1
    hands_on = jnp.logical_and(jnp.logical_and(opens, ahead_ring), y == 1)
    sends_ring = jnp.logical_and(opens, behind_ring)
    beside_lead = jnp.logical_and(gx == 0, jnp.logical_and(az == 1, ta == 0))
    halo_to_lead = jnp.logical_and(gx == 1, az * 4 + ta == 0)
    mine = pl.ds(pl.multiple_of(az * 8, 8), 8)
    own_q = pl.ds(pl.multiple_of(c * 8, 8), 8)

    def device(a, t, g=gx):
        return (g, a, t)

    barrier = pltpu.get_barrier_semaphore()
    across = [lax.rem(az + n, 4) for n in range(4)]
    along = [lax.rem(ta + n, 4) for n in range(4)]
    others = [(across[m], along[n]) for m in range(4) for n in (2, 1, 3, 0) if m + n > 0]

    @pl.when(jnp.logical_not(lead))
    def _():
        for a, t in others:
            pl.semaphore_signal(barrier, inc=1, device_id=device(a, t), device_id_type=MESH)

    def tell(condition, semaphore, block, row=az):
        @pl.when(condition)
        def _():
            pl.semaphore_signal(
                semaphore, inc=1, device_id=device(row, ta, block), device_id_type=MESH
            )

    off_lead = jnp.logical_not(lead)
    second = c == 1
    told = jnp.logical_not(jnp.logical_or(closes, last_block))
    tell(jnp.logical_and(off_lead, told), barrier, gx + 1)
    tell(jnp.logical_and(second, told), barrier, gx + 1, 2 * y)
    for upper in range(2):
        tell(hands_on, barrier, gx + RING, 2 * upper + c)
        tell(hands_on, barrier, up, 2 * upper + c)
        tell(jnp.logical_and(hands_on, c == 0), barrier, up, 2 * upper + 1)
    tell(halo_to_lead, barrier, 0)

    here = [
        pltpu.make_async_copy(vel, vraw, local_sem.at[0]),
        pltpu.make_async_copy(vel.at[pl.ds(8 * c, 8)], vbuf.at[:, mine], local_sem.at[1]),
        pltpu.make_async_copy(pres, pbuf.at[pl.ds(0, 16), own_q], local_sem.at[2]),
    ]
    for number, (source, target) in enumerate(
        [(t_av, av), (t_ap, ap), (t_w, w), (t_wi, wi), (t_b, b), (t_offs, offs)]
    ):
        here.append(pltpu.make_async_copy(source, target, local_sem.at[3 + number]))
    for copy in here:
        copy.start()
    here[0].wait()

    lane8 = lanes_of((8, 128))
    for half in range(2):
        right = jnp.zeros((8, 128), F32)
        left = jnp.zeros((8, 128), F32)
        for j in range(8):
            here_lane = lane8 // 16 == j
            last = vraw[8 * half + j, :, 128:256]
            first = vraw[8 * half + j, :, 0:128]
            right = jnp.where(here_lane, pltpu.roll(last, (16 * j + 16) % 128, 1), right)
            left = jnp.where(here_lane, pltpu.roll(first, 16 * j, 1), left)
        pack[0, half] = right
        pack[1, half] = left

    fv_16[...] = jnp.zeros_like(fv_16)
    fp_16[...] = jnp.zeros_like(fp_16)

    counted = [
        jnp.logical_not(jnp.logical_or(opens, halo_to_lead)),
        jnp.logical_and(jnp.logical_not(opens), c == 0),
        jnp.logical_and(closes, has_down),
        jnp.logical_and(jnp.logical_and(closes, has_down), second),
        sends_ring,
        lead,
    ]
    pl.semaphore_wait(
        barrier, 15 - follows.astype(jnp.int32) + sum(one.astype(jnp.int32) for one in counted)
    )

    @pl.when(lead)
    def _():
        for a, t in others:
            pl.semaphore_signal(there, inc=1, device_id=device(a, t), device_id_type=MESH)

    tell(jnp.logical_and(closes, has_down), ready, down, 2 + c)
    tell(jnp.logical_and(jnp.logical_and(closes, has_down), second), ready, down, 2)
    tell(lead, ready, 1)

    def remote(source, target, send, receive, to):
        return pltpu.make_async_remote_copy(
            src_ref=source, dst_ref=target, send_sem=send, recv_sem=receive,
            device_id=to, device_id_type=MESH,
        )

    def halo_from(source, row, sems):
        return [
            remote(
                source.at[pl.ds(8 * n, 8)], pbuf.at[pl.ds(16 + 8 * n, 8), own_q],
                send_sem.at[sems + n], zrecv.at[n * (1 + c)], device(row + n * (1 - c), ta, up),
            )
            for n in range(2)
        ]

    halo = halo_from(pres, az, 0)
    halo_on = [halo_from(zbuf.at[upper], 2 * upper + c, 18 * (1 - upper)) for upper in range(2)]
    to_ring = [
        remote(
            pres.at[pl.ds(8 * n, 8)], zbuf.at[y, pl.ds(8 * n, 8)],
            send_sem.at[16 + n], ring_recv.at[y, n], device(2 + c, ta, gx - RING),
        )
        for n in range(2)
    ]

    own_half = vel.at[pl.ds(8 * c, 8)]
    other_half = vel.at[pl.ds(8 * other, 8)]
    sends = [
        remote(own_half, vbuf.at[:, mine], send_sem.at[2], vrecv.at[0],
               device(2 * (1 - y) + c, ta)),
        remote(other_half, vbuf.at[:, mine], send_sem.at[3], vrecv.at[1],
               device(2 * (1 - y) + other, ta)),
        remote(other_half, vbuf.at[:, mine], send_sem.at[4], vrecv.at[2],
               device(2 * y + other, ta)),
        remote(pres, pbuf.at[pl.ds(0, 16), own_q], send_sem.at[5], precv.at[0],
               device(2 * y + other, ta)),
    ]
    for a in range(4):
        for side, shift in ((0, 1), (1, 3)):
            sends.append(
                remote(pack.at[side, a % 2], hal.at[side, mine],
                       send_sem.at[6 + 2 * a + side], hrecv.at[side, az],
                       device(a, along[shift]))
            )
    targets = [(2 * (1 - y) + c, ta), (2 * (1 - y) + other, ta)] + [(2 * y + other, ta)] * 2
    targets += [(a, along[shift]) for a in range(4) for shift in (1, 3)]
    to_lead = [jnp.logical_and(gx == 0, a * 4 + t == 0) for a, t in targets]
    def start(numbers):
        for n in numbers:
            @pl.when(jnp.logical_not(to_lead[n]))
            def _():
                sends[n].start()

    start(range(4, 12))
    start((0, 1))

    @pl.when(jnp.logical_not(jnp.logical_or(opens, halo_to_lead)))
    def _():
        for copy in halo:
            copy.start()

    start((3, 2))

    @pl.when(sends_ring)
    def _():
        for copy in to_ring:
            copy.start()

    def send_to_lead():
        pl.semaphore_wait(there, 1)
        for copy, waited_for in zip(sends, to_lead):
            @pl.when(waited_for)
            def _():
                copy.start()

    @pl.when(beside_lead)
    def _():
        send_to_lead()

    for copy in here[3:]:
        copy.wait()
    here[2].wait()
    sends[3].wait_recv()

    def spectra(windows, stations, target, target_16, start):
        count = 16 * stations
        parts = []
        for window in windows:
            cosines = jnp.concatenate([window[:count], window[2 * count:2 * count + 8]], axis=0)
            sines = jnp.concatenate([window[count:2 * count], jnp.zeros((8, 128), F32)], axis=0)
            parts.append(jnp.concatenate([cosines, sines], axis=1))
        spectrum = dot(as_left(jnp.concatenate(parts, axis=0)), w[...])
        for n in range(3):
            rows = spectrum[n * (count + 8):(n + 1) * (count + 8)]
            target[start:start + stations, :, n * 256:(n + 1) * 256] = (
                rows[:count].reshape(stations, 16, 256)
            )
            for part_n in range(2):
                first_row = target_16.shape[0] // 6 * (2 * n + part_n) + start
                target_16[first_row:first_row + stations, 0, :] = (
                    rows[count:count + stations, 128 * part_n:128 * part_n + 128]
                )

    def pressure(chunk):
        rows = pbuf[pl.ds(pl.multiple_of(8 * c + 8 * chunk, 8), 8)].reshape(128, 256)
        modes = dot(ap[...], as_right(rows))
        lane = lanes_of((272, 128))
        first, second = modes[:, :128], modes[:, 128:]
        windows = [
            jnp.where(lane < 96, first, 0.0),
            jnp.where(lane < 32, second, jnp.where(lane >= 96, first, 0.0)),
            jnp.where(lane >= 32, second, 0.0),
        ]
        spectra(windows, 8, fp, fp_16, 8 * chunk)

    def velocity():
        lane = lanes_of((32, 128))
        low = jnp.where(ta > 0, hal[0], 0.0)
        high = jnp.where(ta < 3, hal[1], 0.0)
        for half in range(2):
            columns = [[], [], []]
            for j in range(4 * half, 4 * half + 4):
                first, second = vbuf[j, :, 0:128], vbuf[j, :, 128:256]
                before = pltpu.roll(low, (112 - 16 * j) % 128, 1)
                after = pltpu.roll(high, (128 - 16 * j) % 128, 1)
                columns[0].append(jnp.where(lane < 112, first, before))
                columns[1].append(jnp.where(lane < 64, second, first))
                columns[2].append(jnp.where(lane >= 16, second, after))
            rows = jnp.concatenate([jnp.concatenate(col, axis=0) for col in columns], axis=1)
            modes = dot(av[...], as_right(rows))
            spectra([modes[:, 128 * n:128 * n + 128] for n in range(3)], 4, fv, fv_16, 4 * half)

    pressure(0)

    @pl.when(jnp.logical_and(follows, jnp.logical_not(beside_lead)))
    def _():
        send_to_lead()

    @pl.when(halo_to_lead)
    def _():
        pl.semaphore_wait(ready, 1)
        for copy in halo:
            copy.start()

    onward = remote(
        pbuf.at[pl.ds(16, 8), own_q], pbuf.at[pl.ds(16, 8), own_q],
        send_sem.at[14], relay.at[0], partner_id(gx, y, other, ta),
    )

    def arrived(n):
        pltpu.make_async_copy(
            pres.at[pl.ds(0, 8)], pbuf.at[pl.ds(16, 8), own_q], zrecv.at[n]
        ).wait()

    @pl.when(has_down)
    def _():
        arrived(0)
        onward.start()

    @pl.when(jnp.logical_not(has_down))
    def _():
        pbuf[16:32] = jnp.zeros((16, 16, 256), F32)

    @pl.when(jnp.logical_and(has_down, second))
    def _():
        onward.wait_recv()

    pressure(1)
    here[1].wait()
    for copy in sends[:3]:
        copy.wait_recv()
    for side in range(2):
        for a in range(4):
            pltpu.make_async_copy(
                pack.at[0, 0], hal.at[side, pl.ds(8 * a, 8)], hrecv.at[side, a]
            ).wait()
    velocity()

    @pl.when(jnp.logical_and(has_down, c == 0))
    def _():
        onward.wait_recv()

    @pl.when(jnp.logical_and(has_down, second))
    def _():
        arrived(1)
        arrived(2)

    pressure(2)

    slot = 2 * ta + y

    def station_at(turn):
        ahead = jnp.where(turn < 2, 2, jnp.where(turn < 6, 1 + 2 * (turn % 2), 0))
        core = jnp.where(turn < 2, turn, (turn // 2) % 2)
        core = jnp.where(turn >= 6, turn % 2, core)
        return 4 * core + lax.rem(ta + ahead, 4)

    def target_of(s):
        return device(2 * c + s // 4, s % 4)

    def outgoing(s):
        return remote(part.at[s], recv.at[slot], send2.at[s], recv2.at[slot], target_of(s))

    def deliver(s):
        to_self = jnp.logical_and(y == c, s == 4 * c + ta)

        @pl.when(to_self)
        def _():
            pltpu.make_async_copy(part.at[s], recv.at[slot], recv2.at[slot]).start()

        @pl.when(jnp.logical_not(to_self))
        def _():
            outgoing(s).start()

    def hand_on(n):
        if n == 0:
            pl.semaphore_wait(ready, 4 - 2 * c)
        for upper in (1, 0):
            pltpu.make_async_copy(
                pres.at[pl.ds(8 * n, 8)], zbuf.at[upper, pl.ds(8 * n, 8)], ring_recv.at[upper, n]
            ).wait()
            halo_on[upper][n].start()

    def station(turn):
        s = station_at(turn)
        v = [
            [fv[s, 0:8, 128 * n:128 * n + 128] for n in range(6)],
            [fv[s, 8:16, 128 * n:128 * n + 128] for n in range(6)],
            [fv_16[8 * n + s] for n in range(6)],
        ]
        rows = []
        for k in range(NBR):
            near = s + offs[k]
            real, imag = [], []
            for i in range(3):
                re = im = None
                for n in range(3):
                    vr, vi = v[i][2 * n], v[i][2 * n + 1]
                    if i < 2:
                        pr = fp[near, 8 * i:8 * i + 8, 256 * n:256 * n + 128]
                        pi = fp[near, 8 * i:8 * i + 8, 256 * n + 128:256 * n + 256]
                    else:
                        pr = fp_16[48 * n + near]
                        pi = fp_16[48 * n + 24 + near]
                    one, two = vr * pr + vi * pi, vr * pi - vi * pr
                    re, im = (one, two) if n == 0 else (re + one, im + two)
                real.append(re)
                imag.append(im)
            re = jnp.concatenate([real[0] - imag[2], real[1]], axis=0)
            im = jnp.concatenate([imag[0] + real[2], imag[1]], axis=0)
            rows.append(jnp.concatenate([re, im], axis=1))
        grid = as_left(jnp.concatenate(rows, axis=0))
        part[s] = lax.dot_general(
            wi[...], grid, (((1,), (1,)), ((), ())), preferred_element_type=F32
        )

    def hand_on_at(pair):
        for n, (at_first, elsewhere) in enumerate(HAND_PAIRS):
            @pl.when(jnp.logical_and(hands_on, pair == jnp.where(gx == 0, at_first, elsewhere)))
            def _():
                hand_on(n)

    def stations(pair, carry):
        hand_on_at(pair)
        station(2 * pair)
        station(2 * pair + 1)

        @pl.when(pair > 0)
        def _():
            deliver(station_at(2 * pair - 1))

        deliver(station_at(2 * pair))
        return carry

    lax.fori_loop(0, 4, stations, 0)
    deliver(station_at(7))
    hand_on_at(4)

    for n in range(8):
        pltpu.make_async_copy(part.at[0], recv.at[n], recv2.at[n]).wait()
    sums = []
    for upper in range(2):
        total = recv[upper]
        for n in range(1, 4):
            total = total + recv[2 * n + upper]
        sums.append(total)
    odd = lanes_of((ROWS, 128)) % 2 == 1
    total = sums[0] + jnp.where(odd, -sums[1], sums[1])
    rows_buf[0:ROWS] = dot(as_left(total), b[...])
    for k in range(NBR):
        for n in range(5):
            real = rows_buf[8 * n:8 * n + 8, 128 * (k // 4):128 * (k // 4) + 128]
            imag = rows_buf[LAGS + 8 * n:LAGS + 8 * n + 8, 256 + 128 * (k // 4):384 + 128 * (k // 4)]
            turn_buf[40 * k + 8 * n:40 * k + 8 * n + 8, :] = pltpu.roll(
                real + imag, (128 - 32 * (k % 4)) % 128, 1
            )
    for n in range(9):
        row = turn_buf[pl.ds(4 * n, 8, stride=40), :]
        for j in range(1, 4 if n < 8 else 1):
            turned = pltpu.roll(turn_buf[pl.ds(4 * n + j, 8, stride=40), :], 32 * j, 1)
            row = jnp.where(lane8 // 32 == j, turned, row)
        if n < 8:
            out[0, :, 128 * n:128 * n + 128] = row
        else:
            out[0, :, 1024:1056] = row[:, :32]

    for copy in sends:
        copy.wait_send()

    @pl.when(jnp.logical_not(opens))
    def _():
        for copy in halo:
            copy.wait_send()

    @pl.when(hands_on)
    def _():
        for copy in halo_on[0] + halo_on[1]:
            copy.wait_send()

    @pl.when(sends_ring)
    def _():
        for copy in to_ring:
            copy.wait_send()

    @pl.when(has_down)
    def _():
        onward.wait_send()

    def drain(s, carry):
        @pl.when(jnp.logical_not(jnp.logical_and(y == c, s == 4 * c + ta)))
        def _():
            outgoing(s).wait_send()

        return carry

    lax.fori_loop(0, 8, drain, 0)


def partner_id(gx, y, other, ta):
    return (gx, 2 * y + other, ta)


def solution(mesh):
    groups = mesh.shape["gx"]
    constants = tables()

    def shards(velocity, pressure, offsets):
        any_spec = pl.BlockSpec(memory_space=pltpu.HBM)
        dma = pltpu.SemaphoreType.DMA
        return pl.pallas_call(
            lambda *refs: kernel(groups, *refs),
            out_shape=jax.ShapeDtypeStruct((1, NBR, LAGS * AZIM), F32),
            in_specs=[any_spec] * 8,
            out_specs=pl.BlockSpec(memory_space=pltpu.VMEM),
            scratch_shapes=[
                pltpu.SMEM((NBR,), jnp.int32),
                pltpu.VMEM((8, AZIM, 256), F32),
                pltpu.VMEM((32, 16, 256), F32),
                pltpu.VMEM((2, 16, 8, 256), F32),
                pltpu.VMEM((16, 8, 256), F32),
                pltpu.VMEM((2, 2, 8, 128), F32),
                pltpu.VMEM((2, AZIM, 128), F32),
                *[pltpu.VMEM(table.shape, BF16) for table in constants],
                pltpu.VMEM((8, 16, 768), F32),
                pltpu.VMEM((24, 16, 768), F32),
                pltpu.VMEM((48, 8, 128), F32),
                pltpu.VMEM((144, 8, 128), F32),
                pltpu.VMEM((8, ROWS, 128), F32),
                pltpu.VMEM((8, ROWS, 128), F32),
                pltpu.VMEM((ROWS + 8, 512), F32),
                pltpu.VMEM((40 * NBR, 128), F32),
                dma((9,)), dma((20,)), dma((3,)), dma((1,)), dma((3,)), dma((1,)),
                dma((2, 4)), dma((8,)), dma((8,)),
                dma((2, 2)), *[pltpu.SemaphoreType.REGULAR] * 2,
            ],
            compiler_params=pltpu.CompilerParams(
                collective_id=0, has_side_effects=True, vmem_limit_bytes=48 << 20
            ),
            name="correlate",
        )(*[pltpu.with_memory_space_constraint(x, pltpu.HBM) for x in (velocity, pressure, offsets, *[jnp.asarray(table) for table in constants])])

    return jax.shard_map(
        shards,
        mesh=mesh,
        in_specs=(P("gx", "az", "ta"), P("gx", "az", "ta"), P()),
        out_specs=P(("gx", "az", "ta"), None, None),
        check_vma=False,
    )
```

```python
import math

import jax
import jax.numpy as jnp
import numpy as np
from jax import lax
from jax.experimental import pallas as pl
from jax.experimental.pallas import tpu as pltpu
from jax.sharding import PartitionSpec as P

AZIM = 32
NBR = 8
MAXLAG = 16
LAGS = 33
LEN = 128
RING = 8
HAND_PAIRS = ((2, 0), (4, 4))
ROWS = 72
MESH = pl.DeviceIdType.MESH
F32, BF16 = jnp.float32, jnp.bfloat16


def halves(table):
    high = table.astype(BF16)
    return high, (table - high.astype(np.float32)).astype(BF16)


def tables():
    mode, azim = np.arange(17), np.arange(AZIM)
    angle = 2 * np.pi * ((mode[:, None] * azim[None, :]) % AZIM) / AZIM
    parts = np.stack([np.cos(angle), np.sin(angle)])
    parts[1, 0], parts[1, 16] = 0, 0
    eye = np.eye(8)

    def over_stations(part, stations):
        full = np.einsum("st,cmq->csmtq", np.eye(stations), part)
        depth = stations * part.shape[2]
        main = full[:, :, :16].reshape(2 * stations * 16, depth)
        rest = np.zeros((16, depth))
        rest[:stations] = full[0, :, 16].reshape(stations, depth)
        return np.concatenate([main, rest]).astype(np.float32)

    def left(table):
        high, low = halves(table)
        return np.concatenate([high, high, low], axis=1)

    def right(table):
        high, low = halves(table)
        return np.concatenate([high, high, low], axis=0)

    t = np.arange(LEN)
    omega = 2 * np.pi * ((t[:, None] * t[None, :]) % LEN) / LEN
    cos, sin = np.cos(omega), np.sin(omega)
    time = np.block([[cos, -sin], [-sin, -cos]]).astype(np.float32)
    lag = np.arange(-MAXLAG, MAXLAG + 1)
    omega = 2 * np.pi * ((lag[:, None] * t[None, :]) % LEN) / LEN
    cos, sin = np.cos(omega) / LEN, np.sin(omega) / LEN
    back = np.zeros((ROWS, 2 * LEN), np.float32)
    back[: 2 * LAGS] = np.block([[cos, -sin], [sin, cos]])
    slot = np.arange(16)
    angle = 2 * np.pi * ((slot[:, None] * azim[None, :]) % AZIM) / AZIM
    real, imag = 2 * np.cos(angle), -2 * np.sin(angle)
    real[0], imag[0] = 1, np.where(azim % 2 == 0, 1, -1)
    scale = 1.0 / (AZIM * math.sqrt(AZIM * 1024))
    last = np.concatenate([np.kron(eye, real), np.kron(eye, imag)], axis=1) * scale
    return (
        left(over_stations(parts, 4)),
        left(over_stations(parts[:, :, :16], 8)),
        right(time),
        left(back),
        right(last.astype(np.float32)),
    )


def split(value):
    high = value.astype(BF16)
    return high, (value - high.astype(F32)).astype(BF16)


def as_left(value):
    high, low = split(value)
    return jnp.concatenate([high, low, high], axis=1)


def as_right(value):
    high, low = split(value)
    return jnp.concatenate([high, low, high], axis=0)


def dot(left, right):
    return lax.dot_general(left, right, (((1,), (0,)), ((), ())), preferred_element_type=F32)


def lanes_of(shape):
    return lax.broadcasted_iota(jnp.int32, shape, len(shape) - 1)


def kernel(
    groups, vel, pres, t_offs, t_av, t_ap, t_w, t_wi, t_b, out,
    offs, vbuf, pbuf, zbuf, vraw, pack, hal, av, ap, w, wi, b, fv, fp, fv_16, fp_16, part, recv, rows_buf, turn_buf,
    local_sem, send_sem, vrecv, precv, zrecv, relay, hrecv, send2, recv2, ring_recv, ready, there,
):
    gx, az, ta = lax.axis_index("gx"), lax.axis_index("az"), lax.axis_index("ta")
    y, c = az // 2, az % 2
    other = 1 - c
    partner = {"gx": gx, "az": 2 * y + other, "ta": ta}
    opens = lax.rem(gx, RING) == 0
    closes = lax.rem(gx, RING) == RING - 1
    ahead_ring = gx < groups - RING
    behind_ring = gx >= RING
    up = jnp.where(opens, gx + RING - 1, gx - 1)
    down = jnp.where(closes, gx - RING + 1, gx + 1)
    has_down = gx < groups - 1
    lead = jnp.logical_and(gx == 0, az * 4 + ta == 0)
    follows = jnp.logical_and(gx == 0, az * 4 + ta > 0)
    last_block = gx == groups - 1
    hands_on = jnp.logical_and(jnp.logical_and(opens, ahead_ring), y == 1)
    sends_ring = jnp.logical_and(opens, behind_ring)
    beside_lead = jnp.logical_and(gx == 0, jnp.logical_and(az == 1, ta == 0))
    halo_to_lead = jnp.logical_and(gx == 1, az * 4 + ta == 0)
    mine = pl.ds(pl.multiple_of(az * 8, 8), 8)
    own_q = pl.ds(pl.multiple_of(c * 8, 8), 8)

    def device(a, t, g=gx):
        return (g, a, t)

    barrier = pltpu.get_barrier_semaphore()
    across = [lax.rem(az + n, 4) for n in range(4)]
    along = [lax.rem(ta + n, 4) for n in range(4)]
    others = [(across[m], along[n]) for m in range(4) for n in (2, 1, 3, 0) if m + n > 0]

    @pl.when(jnp.logical_not(lead))
    def _():
        for a, t in others:
            pl.semaphore_signal(barrier, inc=1, device_id=device(a, t), device_id_type=MESH)

    def tell(condition, semaphore, block, row=az):
        @pl.when(condition)
        def _():
            pl.semaphore_signal(
                semaphore, inc=1, device_id=device(row, ta, block), device_id_type=MESH
            )

    off_lead = jnp.logical_not(lead)
    second = c == 1
    told = jnp.logical_not(jnp.logical_or(closes, last_block))
    tell(jnp.logical_and(off_lead, told), barrier, gx + 1)
    tell(jnp.logical_and(second, told), barrier, gx + 1, 2 * y)
    for upper in range(2):
        tell(hands_on, barrier, gx + RING, 2 * upper + c)
        tell(hands_on, barrier, up, 2 * upper + c)
        tell(jnp.logical_and(hands_on, c == 0), barrier, up, 2 * upper + 1)
    tell(halo_to_lead, barrier, 0)

    here = [
        pltpu.make_async_copy(vel, vraw, local_sem.at[0]),
        pltpu.make_async_copy(vel.at[pl.ds(8 * c, 8)], vbuf.at[:, mine], local_sem.at[1]),
        pltpu.make_async_copy(pres, pbuf.at[pl.ds(0, 16), own_q], local_sem.at[2]),
    ]
    for number, (source, target) in enumerate(
        [(t_av, av), (t_ap, ap), (t_w, w), (t_wi, wi), (t_b, b), (t_offs, offs)]
    ):
        here.append(pltpu.make_async_copy(source, target, local_sem.at[3 + number]))
    for copy in here:
        copy.start()
    def remote(source, target, send, receive, to):
        return pltpu.make_async_remote_copy(
            src_ref=source, dst_ref=target, send_sem=send, recv_sem=receive,
            device_id=to, device_id_type=MESH,
        )

    counted = [
        jnp.logical_not(jnp.logical_or(opens, halo_to_lead)),
        jnp.logical_and(jnp.logical_not(opens), c == 0),
        jnp.logical_and(closes, has_down),
        jnp.logical_and(jnp.logical_and(closes, has_down), second),
        sends_ring,
        lead,
    ]
    count = 15 - follows.astype(jnp.int32) + sum(one.astype(jnp.int32) for one in counted)
    own_half = vel.at[pl.ds(8 * c, 8)]
    other_half = vel.at[pl.ds(8 * other, 8)]
    sends = [
        remote(own_half, vbuf.at[:, mine], send_sem.at[2], vrecv.at[0],
               device(2 * (1 - y) + c, ta)),
        remote(other_half, vbuf.at[:, mine], send_sem.at[3], vrecv.at[1],
               device(2 * (1 - y) + other, ta)),
        remote(other_half, vbuf.at[:, mine], send_sem.at[4], vrecv.at[2],
               device(2 * y + other, ta)),
        remote(pres, pbuf.at[pl.ds(0, 16), own_q], send_sem.at[5], precv.at[0],
               device(2 * y + other, ta)),
    ]

    @pl.when(lead)
    def _():
        pl.semaphore_wait(barrier, count)
        for a, t in others:
            pl.semaphore_signal(there, inc=1, device_id=device(a, t), device_id_type=MESH)
        pl.semaphore_signal(ready, inc=1, device_id=device(az, ta, 1), device_id_type=MESH)
        for n in (0, 1, 3, 2):
            sends[n].start()

    here[0].wait()

    lane8 = lanes_of((8, 128))
    for half in range(2):
        right = jnp.zeros((8, 128), F32)
        left = jnp.zeros((8, 128), F32)
        for j in range(8):
            here_lane = lane8 // 16 == j
            last = vraw[8 * half + j, :, 128:256]
            first = vraw[8 * half + j, :, 0:128]
            right = jnp.where(here_lane, pltpu.roll(last, (16 * j + 16) % 128, 1), right)
            left = jnp.where(here_lane, pltpu.roll(first, 16 * j, 1), left)
        pack[0, half] = right
        pack[1, half] = left

    fv_16[...] = jnp.zeros_like(fv_16)
    fp_16[...] = jnp.zeros_like(fp_16)

    @pl.when(off_lead)
    def _():
        pl.semaphore_wait(barrier, count)

    tell(jnp.logical_and(closes, has_down), ready, down, 2 + c)
    tell(jnp.logical_and(jnp.logical_and(closes, has_down), second), ready, down, 2)

    def halo_from(source, row, sems):
        return [
            remote(
                source.at[pl.ds(8 * n, 8)], pbuf.at[pl.ds(16 + 8 * n, 8), own_q],
                send_sem.at[sems + n], zrecv.at[n * (1 + c)], device(row + n * (1 - c), ta, up),
            )
            for n in range(2)
        ]

    halo = halo_from(pres, az, 0)
    halo_on = [halo_from(zbuf.at[upper], 2 * upper + c, 18 * (1 - upper)) for upper in range(2)]
    to_ring = [
        remote(
            pres.at[pl.ds(8 * n, 8)], zbuf.at[y, pl.ds(8 * n, 8)],
            send_sem.at[16 + n], ring_recv.at[y, n], device(2 + c, ta, gx - RING),
        )
        for n in range(2)
    ]

    for a in range(4):
        for side, shift in ((0, 1), (1, 3)):
            sends.append(
                remote(pack.at[side, a % 2], hal.at[side, mine],
                       send_sem.at[6 + 2 * a + side], hrecv.at[side, az],
                       device(a, along[shift]))
            )
    targets = [(2 * (1 - y) + c, ta), (2 * (1 - y) + other, ta)] + [(2 * y + other, ta)] * 2
    targets += [(a, along[shift]) for a in range(4) for shift in (1, 3)]
    to_lead = [jnp.logical_and(gx == 0, a * 4 + t == 0) for a, t in targets]
    def start(numbers):
        for n in numbers:
            begun = lead if n < 4 else False

            @pl.when(jnp.logical_not(jnp.logical_or(to_lead[n], begun)))
            def _():
                sends[n].start()

    start(range(4, 12))
    @pl.when(sends_ring)
    def _():
        to_ring[0].start()

    start((0, 1))

    @pl.when(jnp.logical_not(jnp.logical_or(opens, halo_to_lead)))
    def _():
        for copy in halo:
            copy.start()

    start((3, 2))

    @pl.when(sends_ring)
    def _():
        to_ring[1].start()

    def send_to_lead():
        pl.semaphore_wait(there, 1)
        for copy, waited_for in zip(sends, to_lead):
            @pl.when(waited_for)
            def _():
                copy.start()

    @pl.when(beside_lead)
    def _():
        send_to_lead()

    for copy in here[3:]:
        copy.wait()
    here[2].wait()
    sends[3].wait_recv()

    def spectra(windows, stations, target, target_16, start):
        count = 16 * stations
        parts = []
        for window in windows:
            cosines = jnp.concatenate([window[:count], window[2 * count:2 * count + 8]], axis=0)
            sines = jnp.concatenate([window[count:2 * count], jnp.zeros((8, 128), F32)], axis=0)
            parts.append(jnp.concatenate([cosines, sines], axis=1))
        spectrum = dot(as_left(jnp.concatenate(parts, axis=0)), w[...])
        for n in range(3):
            rows = spectrum[n * (count + 8):(n + 1) * (count + 8)]
            target[start:start + stations, :, n * 256:(n + 1) * 256] = (
                rows[:count].reshape(stations, 16, 256)
            )
            for part_n in range(2):
                first_row = target_16.shape[0] // 6 * (2 * n + part_n) + start
                target_16[first_row:first_row + stations, 0, :] = (
                    rows[count:count + stations, 128 * part_n:128 * part_n + 128]
                )

    def pressure(chunk):
        rows = pbuf[pl.ds(pl.multiple_of(8 * c + 8 * chunk, 8), 8)].reshape(128, 256)
        modes = dot(ap[...], as_right(rows))
        lane = lanes_of((272, 128))
        first, second = modes[:, :128], modes[:, 128:]
        windows = [
            jnp.where(lane < 96, first, 0.0),
            jnp.where(lane < 32, second, jnp.where(lane >= 96, first, 0.0)),
            jnp.where(lane >= 32, second, 0.0),
        ]
        spectra(windows, 8, fp, fp_16, 8 * chunk)

    def velocity():
        lane = lanes_of((32, 128))
        low = jnp.where(ta > 0, hal[0], 0.0)
        high = jnp.where(ta < 3, hal[1], 0.0)
        for half in range(2):
            columns = [[], [], []]
            for j in range(4 * half, 4 * half + 4):
                first, second = vbuf[j, :, 0:128], vbuf[j, :, 128:256]
                before = pltpu.roll(low, (112 - 16 * j) % 128, 1)
                after = pltpu.roll(high, (128 - 16 * j) % 128, 1)
                columns[0].append(jnp.where(lane < 112, first, before))
                columns[1].append(jnp.where(lane < 64, second, first))
                columns[2].append(jnp.where(lane >= 16, second, after))
            rows = jnp.concatenate([jnp.concatenate(col, axis=0) for col in columns], axis=1)
            modes = dot(av[...], as_right(rows))
            spectra([modes[:, 128 * n:128 * n + 128] for n in range(3)], 4, fv, fv_16, 4 * half)

    pressure(0)

    @pl.when(jnp.logical_and(follows, jnp.logical_not(beside_lead)))
    def _():
        send_to_lead()

    @pl.when(halo_to_lead)
    def _():
        pl.semaphore_wait(ready, 1)
        for copy in halo:
            copy.start()

    onward = remote(
        pbuf.at[pl.ds(16, 8), own_q], pbuf.at[pl.ds(16, 8), own_q],
        send_sem.at[14], relay.at[0], partner_id(gx, y, other, ta),
    )

    def arrived(n):
        pltpu.make_async_copy(
            pres.at[pl.ds(0, 8)], pbuf.at[pl.ds(16, 8), own_q], zrecv.at[n]
        ).wait()

    @pl.when(has_down)
    def _():
        arrived(0)
        onward.start()

    @pl.when(jnp.logical_not(has_down))
    def _():
        pbuf[16:32] = jnp.zeros((16, 16, 256), F32)

    @pl.when(jnp.logical_and(has_down, second))
    def _():
        onward.wait_recv()

    pressure(1)
    here[1].wait()
    for copy in sends[:3]:
        copy.wait_recv()
    for side in range(2):
        for a in range(4):
            pltpu.make_async_copy(
                pack.at[0, 0], hal.at[side, pl.ds(8 * a, 8)], hrecv.at[side, a]
            ).wait()
    velocity()

    @pl.when(jnp.logical_and(has_down, c == 0))
    def _():
        onward.wait_recv()

    @pl.when(jnp.logical_and(has_down, second))
    def _():
        arrived(1)
        arrived(2)

    pressure(2)

    slot = 2 * ta + y

    def station_at(turn):
        ahead = jnp.where(turn < 2, 2, jnp.where(turn < 6, 1 + 2 * (turn % 2), 0))
        core = jnp.where(turn < 2, turn, (turn // 2) % 2)
        core = jnp.where(turn >= 6, turn % 2, core)
        return 4 * core + lax.rem(ta + ahead, 4)

    def target_of(s):
        return device(2 * c + s // 4, s % 4)

    def outgoing(s):
        return remote(part.at[s], recv.at[slot], send2.at[s], recv2.at[slot], target_of(s))

    def deliver(s):
        to_self = jnp.logical_and(y == c, s == 4 * c + ta)

        @pl.when(to_self)
        def _():
            pltpu.make_async_copy(part.at[s], recv.at[slot], recv2.at[slot]).start()

        @pl.when(jnp.logical_not(to_self))
        def _():
            outgoing(s).start()

    def hand_on(n):
        if n == 0:
            pl.semaphore_wait(ready, 4 - 2 * c)
        for upper in (1, 0):
            pltpu.make_async_copy(
                pres.at[pl.ds(8 * n, 8)], zbuf.at[upper, pl.ds(8 * n, 8)], ring_recv.at[upper, n]
            ).wait()
            halo_on[upper][n].start()

    def station(turn):
        s = station_at(turn)
        v = [
            [fv[s, 0:8, 128 * n:128 * n + 128] for n in range(6)],
            [fv[s, 8:16, 128 * n:128 * n + 128] for n in range(6)],
            [fv_16[8 * n + s] for n in range(6)],
        ]
        rows = []
        for k in range(NBR):
            near = s + offs[k]
            real, imag = [], []
            for i in range(3):
                re = im = None
                for n in range(3):
                    vr, vi = v[i][2 * n], v[i][2 * n + 1]
                    if i < 2:
                        pr = fp[near, 8 * i:8 * i + 8, 256 * n:256 * n + 128]
                        pi = fp[near, 8 * i:8 * i + 8, 256 * n + 128:256 * n + 256]
                    else:
                        pr = fp_16[48 * n + near]
                        pi = fp_16[48 * n + 24 + near]
                    one, two = vr * pr + vi * pi, vr * pi - vi * pr
                    re, im = (one, two) if n == 0 else (re + one, im + two)
                real.append(re)
                imag.append(im)
            re = jnp.concatenate([real[0] - imag[2], real[1]], axis=0)
            im = jnp.concatenate([imag[0] + real[2], imag[1]], axis=0)
            rows.append(jnp.concatenate([re, im], axis=1))
        grid = as_left(jnp.concatenate(rows, axis=0))
        part[s] = lax.dot_general(
            wi[...], grid, (((1,), (1,)), ((), ())), preferred_element_type=F32
        )

    def hand_on_at(pair):
        for n, (at_first, elsewhere) in enumerate(HAND_PAIRS):
            @pl.when(jnp.logical_and(hands_on, pair == jnp.where(gx == 0, at_first, elsewhere)))
            def _():
                hand_on(n)

    def stations(pair, carry):
        hand_on_at(pair)
        station(2 * pair)
        station(2 * pair + 1)

        @pl.when(pair > 0)
        def _():
            deliver(station_at(2 * pair - 1))

        deliver(station_at(2 * pair))
        return carry

    lax.fori_loop(0, 4, stations, 0)
    deliver(station_at(7))
    hand_on_at(4)

    for n in range(8):
        pltpu.make_async_copy(part.at[0], recv.at[n], recv2.at[n]).wait()
    sums = []
    for upper in range(2):
        total = recv[upper]
        for n in range(1, 4):
            total = total + recv[2 * n + upper]
        sums.append(total)
    odd = lanes_of((ROWS, 128)) % 2 == 1
    total = sums[0] + jnp.where(odd, -sums[1], sums[1])
    rows_buf[0:ROWS] = dot(as_left(total), b[...])
    for k in range(NBR):
        for n in range(5):
            real = rows_buf[8 * n:8 * n + 8, 128 * (k // 4):128 * (k // 4) + 128]
            imag = rows_buf[LAGS + 8 * n:LAGS + 8 * n + 8, 256 + 128 * (k // 4):384 + 128 * (k // 4)]
            turn_buf[40 * k + 8 * n:40 * k + 8 * n + 8, :] = pltpu.roll(
                real + imag, (128 - 32 * (k % 4)) % 128, 1
            )
    for n in range(9):
        row = turn_buf[pl.ds(4 * n, 8, stride=40), :]
        for j in range(1, 4 if n < 8 else 1):
            turned = pltpu.roll(turn_buf[pl.ds(4 * n + j, 8, stride=40), :], 32 * j, 1)
            row = jnp.where(lane8 // 32 == j, turned, row)
        if n < 8:
            out[0, :, 128 * n:128 * n + 128] = row
        else:
            out[0, :, 1024:1056] = row[:, :32]

    for copy in sends:
        copy.wait_send()

    @pl.when(jnp.logical_not(opens))
    def _():
        for copy in halo:
            copy.wait_send()

    @pl.when(hands_on)
    def _():
        for copy in halo_on[0] + halo_on[1]:
            copy.wait_send()

    @pl.when(sends_ring)
    def _():
        for copy in to_ring:
            copy.wait_send()

    @pl.when(has_down)
    def _():
        onward.wait_send()

    def drain(s, carry):
        @pl.when(jnp.logical_not(jnp.logical_and(y == c, s == 4 * c + ta)))
        def _():
            outgoing(s).wait_send()

        return carry

    lax.fori_loop(0, 8, drain, 0)


def partner_id(gx, y, other, ta):
    return (gx, 2 * y + other, ta)


def solution(mesh):
    groups = mesh.shape["gx"]
    constants = tables()

    def shards(velocity, pressure, offsets):
        any_spec = pl.BlockSpec(memory_space=pltpu.HBM)
        dma = pltpu.SemaphoreType.DMA
        return pl.pallas_call(
            lambda *refs: kernel(groups, *refs),
            out_shape=jax.ShapeDtypeStruct((1, NBR, LAGS * AZIM), F32),
            in_specs=[any_spec] * 8,
            out_specs=pl.BlockSpec(memory_space=pltpu.VMEM),
            scratch_shapes=[
                pltpu.SMEM((NBR,), jnp.int32),
                pltpu.VMEM((8, AZIM, 256), F32),
                pltpu.VMEM((32, 16, 256), F32),
                pltpu.VMEM((2, 16, 8, 256), F32),
                pltpu.VMEM((16, 8, 256), F32),
                pltpu.VMEM((2, 2, 8, 128), F32),
                pltpu.VMEM((2, AZIM, 128), F32),
                *[pltpu.VMEM(table.shape, BF16) for table in constants],
                pltpu.VMEM((8, 16, 768), F32),
                pltpu.VMEM((24, 16, 768), F32),
                pltpu.VMEM((48, 8, 128), F32),
                pltpu.VMEM((144, 8, 128), F32),
                pltpu.VMEM((8, ROWS, 128), F32),
                pltpu.VMEM((8, ROWS, 128), F32),
                pltpu.VMEM((ROWS + 8, 512), F32),
                pltpu.VMEM((40 * NBR, 128), F32),
                dma((9,)), dma((20,)), dma((3,)), dma((1,)), dma((3,)), dma((1,)),
                dma((2, 4)), dma((8,)), dma((8,)),
                dma((2, 2)), *[pltpu.SemaphoreType.REGULAR] * 2,
            ],
            compiler_params=pltpu.CompilerParams(
                collective_id=0, has_side_effects=True, vmem_limit_bytes=48 << 20
            ),
            name="correlate",
        )(*[pltpu.with_memory_space_constraint(x, pltpu.HBM) for x in (velocity, pressure, offsets, *[jnp.asarray(table) for table in constants])])

    return jax.shard_map(
        shards,
        mesh=mesh,
        in_specs=(P("gx", "az", "ta"), P("gx", "az", "ta"), P()),
        out_specs=P(("gx", "az", "ta"), None, None),
        check_vma=False,
    )
```

```python
import math

import jax
import jax.numpy as jnp
import numpy as np
from jax import lax
from jax.experimental import pallas as pl
from jax.experimental.pallas import tpu as pltpu
from jax.sharding import PartitionSpec as P

AZIM = 32
NBR = 8
MAXLAG = 16
LAGS = 33
LEN = 128
RING = 8
HAND_PAIRS = ((2, 0), (4, 4))
ROWS = 66
MESH = pl.DeviceIdType.MESH
F32, BF16 = jnp.float32, jnp.bfloat16


def halves(table):
    high = table.astype(BF16)
    return high, (table - high.astype(np.float32)).astype(BF16)


def tables():
    mode, azim = np.arange(17), np.arange(AZIM)
    angle = 2 * np.pi * ((mode[:, None] * azim[None, :]) % AZIM) / AZIM
    parts = np.stack([np.cos(angle), np.sin(angle)])
    parts[1, 0], parts[1, 16] = 0, 0
    eye = np.eye(8)

    def over_stations(part, stations):
        full = np.einsum("st,cmq->csmtq", np.eye(stations), part)
        depth = stations * part.shape[2]
        main = full[:, :, :16].reshape(2 * stations * 16, depth)
        rest = np.zeros((16, depth))
        rest[:stations] = full[0, :, 16].reshape(stations, depth)
        return np.concatenate([main, rest]).astype(np.float32)

    def left(table):
        high, low = halves(table)
        return np.concatenate([high, high, low], axis=1)

    def right(table):
        high, low = halves(table)
        return np.concatenate([high, high, low], axis=0)

    t = np.arange(LEN)
    omega = 2 * np.pi * ((t[:, None] * t[None, :]) % LEN) / LEN
    cos, sin = np.cos(omega), np.sin(omega)
    time = np.block([[cos, -sin], [-sin, -cos]]).astype(np.float32)
    lag = np.arange(-MAXLAG, MAXLAG + 1)
    omega = 2 * np.pi * ((lag[:, None] * t[None, :]) % LEN) / LEN
    cos, sin = np.cos(omega) / LEN, np.sin(omega) / LEN
    back = np.zeros((ROWS, 2 * LEN), np.float32)
    back[: 2 * LAGS] = np.block([[cos, -sin], [sin, cos]])
    slot = np.arange(16)
    angle = 2 * np.pi * ((slot[:, None] * azim[None, :]) % AZIM) / AZIM
    real, imag = 2 * np.cos(angle), -2 * np.sin(angle)
    real[0], imag[0] = 1, np.where(azim % 2 == 0, 1, -1)
    scale = 1.0 / (AZIM * math.sqrt(AZIM * 1024))
    last = np.concatenate([np.kron(eye, real), np.kron(eye, imag)], axis=1) * scale
    return (
        left(over_stations(parts, 4)),
        left(over_stations(parts[:, :, :16], 8)),
        right(time),
        left(back),
        right(last.astype(np.float32)),
    )


def split(value):
    high = value.astype(BF16)
    return high, (value - high.astype(F32)).astype(BF16)


def as_left(value):
    high, low = split(value)
    return jnp.concatenate([high, low, high], axis=1)


def as_right(value):
    high, low = split(value)
    return jnp.concatenate([high, low, high], axis=0)


def dot(left, right):
    return lax.dot_general(left, right, (((1,), (0,)), ((), ())), preferred_element_type=F32)


def lanes_of(shape):
    return lax.broadcasted_iota(jnp.int32, shape, len(shape) - 1)


def kernel(
    groups, vel, pres, t_offs, t_av, t_ap, t_w, t_wi, t_b, out,
    offs, vbuf, pbuf, zbuf, vraw, pack, hal, av, ap, w, wi, b, fv, fp, fv_16, fp_16, part, recv, rows_buf, turn_buf,
    local_sem, send_sem, vrecv, precv, zrecv, relay, hrecv, send2, recv2, ring_recv, ready, there,
):
    gx, az, ta = lax.axis_index("gx"), lax.axis_index("az"), lax.axis_index("ta")
    y, c = az // 2, az % 2
    other = 1 - c
    partner = {"gx": gx, "az": 2 * y + other, "ta": ta}
    opens = lax.rem(gx, RING) == 0
    closes = lax.rem(gx, RING) == RING - 1
    ahead_ring = gx < groups - RING
    behind_ring = gx >= RING
    up = jnp.where(opens, gx + RING - 1, gx - 1)
    down = jnp.where(closes, gx - RING + 1, gx + 1)
    has_down = gx < groups - 1
    lead = jnp.logical_and(gx == 0, az * 4 + ta == 0)
    follows = jnp.logical_and(gx == 0, az * 4 + ta > 0)
    last_block = gx == groups - 1
    hands_on = jnp.logical_and(jnp.logical_and(opens, ahead_ring), y == 1)
    sends_ring = jnp.logical_and(opens, behind_ring)
    beside_lead = jnp.logical_and(gx == 0, jnp.logical_and(az == 1, ta == 0))
    halo_to_lead = jnp.logical_and(gx == 1, az * 4 + ta == 0)
    mine = pl.ds(pl.multiple_of(az * 8, 8), 8)
    own_q = pl.ds(pl.multiple_of(c * 8, 8), 8)

    def device(a, t, g=gx):
        return (g, a, t)

    barrier = pltpu.get_barrier_semaphore()
    across = [lax.rem(az + n, 4) for n in range(4)]
    along = [lax.rem(ta + n, 4) for n in range(4)]
    others = [(across[m], along[n]) for m in range(4) for n in (2, 1, 3, 0) if m + n > 0]

    @pl.when(jnp.logical_not(lead))
    def _():
        for a, t in others:
            pl.semaphore_signal(barrier, inc=1, device_id=device(a, t), device_id_type=MESH)

    def tell(condition, semaphore, block, row=az):
        @pl.when(condition)
        def _():
            pl.semaphore_signal(
                semaphore, inc=1, device_id=device(row, ta, block), device_id_type=MESH
            )

    off_lead = jnp.logical_not(lead)
    second = c == 1
    told = jnp.logical_not(jnp.logical_or(closes, last_block))
    tell(jnp.logical_and(off_lead, told), barrier, gx + 1)
    tell(jnp.logical_and(second, told), barrier, gx + 1, 2 * y)
    for upper in range(2):
        tell(hands_on, barrier, gx + RING, 2 * upper + c)
        tell(hands_on, barrier, up, 2 * upper + c)
        tell(jnp.logical_and(hands_on, c == 0), barrier, up, 2 * upper + 1)
    tell(halo_to_lead, barrier, 0)

    here = [
        pltpu.make_async_copy(vel, vraw, local_sem.at[0]),
        pltpu.make_async_copy(vel.at[pl.ds(8 * c, 8)], vbuf.at[:, mine], local_sem.at[1]),
        pltpu.make_async_copy(pres, pbuf.at[pl.ds(0, 16), own_q], local_sem.at[2]),
    ]
    for number, (source, target) in enumerate(
        [(t_av, av), (t_ap, ap), (t_w, w), (t_wi, wi), (t_b, b), (t_offs, offs)]
    ):
        here.append(pltpu.make_async_copy(source, target, local_sem.at[3 + number]))
    for copy in here:
        copy.start()
    def remote(source, target, send, receive, to):
        return pltpu.make_async_remote_copy(
            src_ref=source, dst_ref=target, send_sem=send, recv_sem=receive,
            device_id=to, device_id_type=MESH,
        )

    counted = [
        jnp.logical_not(jnp.logical_or(opens, halo_to_lead)),
        jnp.logical_and(jnp.logical_not(opens), c == 0),
        jnp.logical_and(closes, has_down),
        jnp.logical_and(jnp.logical_and(closes, has_down), second),
        sends_ring,
        lead,
    ]
    count = 15 - follows.astype(jnp.int32) + sum(one.astype(jnp.int32) for one in counted)
    own_half = vel.at[pl.ds(8 * c, 8)]
    other_half = vel.at[pl.ds(8 * other, 8)]
    sends = [
        remote(own_half, vbuf.at[:, mine], send_sem.at[2], vrecv.at[0],
               device(2 * (1 - y) + c, ta)),
        remote(other_half, vbuf.at[:, mine], send_sem.at[3], vrecv.at[1],
               device(2 * (1 - y) + other, ta)),
        remote(other_half, vbuf.at[:, mine], send_sem.at[4], vrecv.at[2],
               device(2 * y + other, ta)),
        remote(pres, pbuf.at[pl.ds(0, 16), own_q], send_sem.at[5], precv.at[0],
               device(2 * y + other, ta)),
    ]

    @pl.when(lead)
    def _():
        pl.semaphore_wait(barrier, count)
        for a, t in others:
            pl.semaphore_signal(there, inc=1, device_id=device(a, t), device_id_type=MESH)
        pl.semaphore_signal(ready, inc=1, device_id=device(az, ta, 1), device_id_type=MESH)
        for n in (0, 1, 3, 2):
            sends[n].start()

    here[0].wait()

    lane8 = lanes_of((8, 128))
    for half in range(2):
        right = jnp.zeros((8, 128), F32)
        left = jnp.zeros((8, 128), F32)
        for j in range(8):
            here_lane = lane8 // 16 == j
            last = vraw[8 * half + j, :, 128:256]
            first = vraw[8 * half + j, :, 0:128]
            right = jnp.where(here_lane, pltpu.roll(last, (16 * j + 16) % 128, 1), right)
            left = jnp.where(here_lane, pltpu.roll(first, 16 * j, 1), left)
        pack[0, half] = right
        pack[1, half] = left

    fv_16[...] = jnp.zeros_like(fv_16)
    fp_16[...] = jnp.zeros_like(fp_16)

    @pl.when(off_lead)
    def _():
        pl.semaphore_wait(barrier, count)

    tell(jnp.logical_and(closes, has_down), ready, down, 2 + c)
    tell(jnp.logical_and(jnp.logical_and(closes, has_down), second), ready, down, 2)

    def halo_from(source, row, sems):
        return [
            remote(
                source.at[pl.ds(8 * n, 8)], pbuf.at[pl.ds(16 + 8 * n, 8), own_q],
                send_sem.at[sems + n], zrecv.at[n * (1 + c)], device(row + n * (1 - c), ta, up),
            )
            for n in range(2)
        ]

    halo = halo_from(pres, az, 0)
    halo_on = [halo_from(zbuf.at[upper], 2 * upper + c, 18 * (1 - upper)) for upper in range(2)]
    to_ring = [
        remote(
            pres.at[pl.ds(8 * n, 8)], zbuf.at[y, pl.ds(8 * n, 8)],
            send_sem.at[16 + n], ring_recv.at[y, n], device(2 + c, ta, gx - RING),
        )
        for n in range(2)
    ]

    for a in range(4):
        for side, shift in ((0, 1), (1, 3)):
            sends.append(
                remote(pack.at[side, a % 2], hal.at[side, mine],
                       send_sem.at[6 + 2 * a + side], hrecv.at[side, az],
                       device(a, along[shift]))
            )
    targets = [(2 * (1 - y) + c, ta), (2 * (1 - y) + other, ta)] + [(2 * y + other, ta)] * 2
    targets += [(a, along[shift]) for a in range(4) for shift in (1, 3)]
    to_lead = [jnp.logical_and(gx == 0, a * 4 + t == 0) for a, t in targets]
    def start(numbers):
        for n in numbers:
            begun = lead if n < 4 else False

            @pl.when(jnp.logical_not(jnp.logical_or(to_lead[n], begun)))
            def _():
                sends[n].start()

    start(range(4, 12))
    @pl.when(sends_ring)
    def _():
        to_ring[0].start()

    start((0, 1))

    @pl.when(jnp.logical_not(jnp.logical_or(opens, halo_to_lead)))
    def _():
        for copy in halo:
            copy.start()

    start((3, 2))

    @pl.when(sends_ring)
    def _():
        to_ring[1].start()

    def send_to_lead():
        pl.semaphore_wait(there, 1)
        for copy, waited_for in zip(sends, to_lead):
            @pl.when(waited_for)
            def _():
                copy.start()

    @pl.when(beside_lead)
    def _():
        send_to_lead()

    for copy in here[3:]:
        copy.wait()
    here[2].wait()
    sends[3].wait_recv()

    def spectra(windows, stations, target, target_16, start):
        count = 16 * stations
        parts = []
        for window in windows:
            cosines = jnp.concatenate([window[:count], window[2 * count:2 * count + 8]], axis=0)
            sines = jnp.concatenate([window[count:2 * count], jnp.zeros((8, 128), F32)], axis=0)
            parts.append(jnp.concatenate([cosines, sines], axis=1))
        spectrum = dot(as_left(jnp.concatenate(parts, axis=0)), w[...])
        for n in range(3):
            rows = spectrum[n * (count + 8):(n + 1) * (count + 8)]
            target[start:start + stations, :, n * 256:(n + 1) * 256] = (
                rows[:count].reshape(stations, 16, 256)
            )
            for part_n in range(2):
                first_row = target_16.shape[0] // 6 * (2 * n + part_n) + start
                target_16[first_row:first_row + stations, 0, :] = (
                    rows[count:count + stations, 128 * part_n:128 * part_n + 128]
                )

    def pressure(chunk):
        rows = pbuf[pl.ds(pl.multiple_of(8 * c + 8 * chunk, 8), 8)].reshape(128, 256)
        modes = dot(ap[...], as_right(rows))
        lane = lanes_of((272, 128))
        first, second = modes[:, :128], modes[:, 128:]
        windows = [
            jnp.where(lane < 96, first, 0.0),
            jnp.where(lane < 32, second, jnp.where(lane >= 96, first, 0.0)),
            jnp.where(lane >= 32, second, 0.0),
        ]
        spectra(windows, 8, fp, fp_16, 8 * chunk)

    def velocity():
        lane = lanes_of((32, 128))
        low = jnp.where(ta > 0, hal[0], 0.0)
        high = jnp.where(ta < 3, hal[1], 0.0)
        for half in range(2):
            columns = [[], [], []]
            for j in range(4 * half, 4 * half + 4):
                first, second = vbuf[j, :, 0:128], vbuf[j, :, 128:256]
                before = pltpu.roll(low, (112 - 16 * j) % 128, 1)
                after = pltpu.roll(high, (128 - 16 * j) % 128, 1)
                columns[0].append(jnp.where(lane < 112, first, before))
                columns[1].append(jnp.where(lane < 64, second, first))
                columns[2].append(jnp.where(lane >= 16, second, after))
            rows = jnp.concatenate([jnp.concatenate(col, axis=0) for col in columns], axis=1)
            modes = dot(av[...], as_right(rows))
            spectra([modes[:, 128 * n:128 * n + 128] for n in range(3)], 4, fv, fv_16, 4 * half)

    pressure(0)

    @pl.when(jnp.logical_and(follows, jnp.logical_not(beside_lead)))
    def _():
        send_to_lead()

    @pl.when(halo_to_lead)
    def _():
        pl.semaphore_wait(ready, 1)
        for copy in halo:
            copy.start()

    onward = remote(
        pbuf.at[pl.ds(16, 8), own_q], pbuf.at[pl.ds(16, 8), own_q],
        send_sem.at[14], relay.at[0], partner_id(gx, y, other, ta),
    )

    def arrived(n):
        pltpu.make_async_copy(
            pres.at[pl.ds(0, 8)], pbuf.at[pl.ds(16, 8), own_q], zrecv.at[n]
        ).wait()

    @pl.when(has_down)
    def _():
        arrived(0)
        onward.start()

    @pl.when(jnp.logical_not(has_down))
    def _():
        pbuf[16:32] = jnp.zeros((16, 16, 256), F32)

    @pl.when(jnp.logical_and(has_down, second))
    def _():
        onward.wait_recv()

    pressure(1)
    here[1].wait()
    for copy in sends[:3]:
        copy.wait_recv()
    for side in range(2):
        for a in range(4):
            pltpu.make_async_copy(
                pack.at[0, 0], hal.at[side, pl.ds(8 * a, 8)], hrecv.at[side, a]
            ).wait()
    velocity()

    @pl.when(jnp.logical_and(has_down, c == 0))
    def _():
        onward.wait_recv()

    @pl.when(jnp.logical_and(has_down, second))
    def _():
        arrived(1)
        arrived(2)

    pressure(2)

    slot = 2 * ta + y

    def station_at(turn):
        ahead = jnp.where(turn < 2, 2, jnp.where(turn < 6, 1 + 2 * (turn % 2), 0))
        core = jnp.where(turn < 2, turn, (turn // 2) % 2)
        core = jnp.where(turn >= 6, turn % 2, core)
        return 4 * core + lax.rem(ta + ahead, 4)

    def target_of(s):
        return device(2 * c + s // 4, s % 4)

    def outgoing(s):
        return remote(part.at[s], recv.at[slot], send2.at[s], recv2.at[slot], target_of(s))

    def deliver(s):
        to_self = jnp.logical_and(y == c, s == 4 * c + ta)

        @pl.when(to_self)
        def _():
            pltpu.make_async_copy(part.at[s], recv.at[slot], recv2.at[slot]).start()

        @pl.when(jnp.logical_not(to_self))
        def _():
            outgoing(s).start()

    def hand_on(n):
        if n == 0:
            pl.semaphore_wait(ready, 4 - 2 * c)
        for upper in (1, 0):
            pltpu.make_async_copy(
                pres.at[pl.ds(8 * n, 8)], zbuf.at[upper, pl.ds(8 * n, 8)], ring_recv.at[upper, n]
            ).wait()
            halo_on[upper][n].start()

    def station(turn):
        s = station_at(turn)
        v = [
            [fv[s, 0:8, 128 * n:128 * n + 128] for n in range(6)],
            [fv[s, 8:16, 128 * n:128 * n + 128] for n in range(6)],
            [fv_16[8 * n + s] for n in range(6)],
        ]
        rows = []
        for k in range(NBR):
            near = s + offs[k]
            real, imag = [], []
            for i in range(3):
                re = im = None
                for n in range(3):
                    vr, vi = v[i][2 * n], v[i][2 * n + 1]
                    if i < 2:
                        pr = fp[near, 8 * i:8 * i + 8, 256 * n:256 * n + 128]
                        pi = fp[near, 8 * i:8 * i + 8, 256 * n + 128:256 * n + 256]
                    else:
                        pr = fp_16[48 * n + near]
                        pi = fp_16[48 * n + 24 + near]
                    one, two = vr * pr + vi * pi, vr * pi - vi * pr
                    re, im = (one, two) if n == 0 else (re + one, im + two)
                real.append(re)
                imag.append(im)
            re = jnp.concatenate([real[0] - imag[2], real[1]], axis=0)
            im = jnp.concatenate([imag[0] + real[2], imag[1]], axis=0)
            rows.append(jnp.concatenate([re, im], axis=1))
        grid = as_left(jnp.concatenate(rows, axis=0))
        part[s] = lax.dot_general(
            wi[...], grid, (((1,), (1,)), ((), ())), preferred_element_type=F32
        )

    def hand_on_at(pair):
        for n, (at_first, elsewhere) in enumerate(HAND_PAIRS):
            @pl.when(jnp.logical_and(hands_on, pair == jnp.where(gx == 0, at_first, elsewhere)))
            def _():
                hand_on(n)

    def stations(pair, carry):
        hand_on_at(pair)
        station(2 * pair)
        station(2 * pair + 1)

        @pl.when(pair > 0)
        def _():
            deliver(station_at(2 * pair - 1))

        deliver(station_at(2 * pair))
        return carry

    lax.fori_loop(0, 4, stations, 0)
    deliver(station_at(7))
    hand_on_at(4)

    for n in range(8):
        pltpu.make_async_copy(part.at[0], recv.at[n], recv2.at[n]).wait()
    sums = []
    for upper in range(2):
        total = recv[upper]
        for n in range(1, 4):
            total = total + recv[2 * n + upper]
        sums.append(total)
    odd = lanes_of((ROWS, 128)) % 2 == 1
    total = sums[0] + jnp.where(odd, -sums[1], sums[1])
    rows_buf[0:ROWS] = dot(as_left(total), b[...])
    for k in range(NBR):
        for n in range(5):
            real = rows_buf[8 * n:8 * n + 8, 128 * (k // 4):128 * (k // 4) + 128]
            imag = rows_buf[LAGS + 8 * n:LAGS + 8 * n + 8, 256 + 128 * (k // 4):384 + 128 * (k // 4)]
            turn_buf[40 * k + 8 * n:40 * k + 8 * n + 8, :] = pltpu.roll(
                real + imag, (128 - 32 * (k % 4)) % 128, 1
            )
    for n in range(9):
        row = turn_buf[pl.ds(4 * n, 8, stride=40), :]
        for j in range(1, 4 if n < 8 else 1):
            turned = pltpu.roll(turn_buf[pl.ds(4 * n + j, 8, stride=40), :], 32 * j, 1)
            row = jnp.where(lane8 // 32 == j, turned, row)
        if n < 8:
            out[0, :, 128 * n:128 * n + 128] = row
        else:
            out[0, :, 1024:1056] = row[:, :32]

    for copy in sends:
        copy.wait_send()

    @pl.when(jnp.logical_not(opens))
    def _():
        for copy in halo:
            copy.wait_send()

    @pl.when(hands_on)
    def _():
        for copy in halo_on[0] + halo_on[1]:
            copy.wait_send()

    @pl.when(sends_ring)
    def _():
        for copy in to_ring:
            copy.wait_send()

    @pl.when(has_down)
    def _():
        onward.wait_send()

    def drain(s, carry):
        @pl.when(jnp.logical_not(jnp.logical_and(y == c, s == 4 * c + ta)))
        def _():
            outgoing(s).wait_send()

        return carry

    lax.fori_loop(0, 8, drain, 0)


def partner_id(gx, y, other, ta):
    return (gx, 2 * y + other, ta)


def solution(mesh):
    groups = mesh.shape["gx"]
    constants = tables()

    def shards(velocity, pressure, offsets):
        any_spec = pl.BlockSpec(memory_space=pltpu.HBM)
        dma = pltpu.SemaphoreType.DMA
        return pl.pallas_call(
            lambda *refs: kernel(groups, *refs),
            out_shape=jax.ShapeDtypeStruct((1, NBR, LAGS * AZIM), F32),
            in_specs=[any_spec] * 8,
            out_specs=pl.BlockSpec(memory_space=pltpu.VMEM),
            scratch_shapes=[
                pltpu.SMEM((NBR,), jnp.int32),
                pltpu.VMEM((8, AZIM, 256), F32),
                pltpu.VMEM((32, 16, 256), F32),
                pltpu.VMEM((2, 16, 8, 256), F32),
                pltpu.VMEM((16, 8, 256), F32),
                pltpu.VMEM((2, 2, 8, 128), F32),
                pltpu.VMEM((2, AZIM, 128), F32),
                *[pltpu.VMEM(table.shape, BF16) for table in constants],
                pltpu.VMEM((8, 16, 768), F32),
                pltpu.VMEM((24, 16, 768), F32),
                pltpu.VMEM((48, 8, 128), F32),
                pltpu.VMEM((144, 8, 128), F32),
                pltpu.VMEM((8, ROWS, 128), F32),
                pltpu.VMEM((8, ROWS, 128), F32),
                pltpu.VMEM((ROWS + 8, 512), F32),
                pltpu.VMEM((40 * NBR, 128), F32),
                dma((9,)), dma((20,)), dma((3,)), dma((1,)), dma((3,)), dma((1,)),
                dma((2, 4)), dma((8,)), dma((8,)),
                dma((2, 2)), *[pltpu.SemaphoreType.REGULAR] * 2,
            ],
            compiler_params=pltpu.CompilerParams(
                collective_id=0, has_side_effects=True, vmem_limit_bytes=48 << 20
            ),
            name="correlate",
        )(*[pltpu.with_memory_space_constraint(x, pltpu.HBM) for x in (velocity, pressure, offsets, *[jnp.asarray(table) for table in constants])])

    return jax.shard_map(
        shards,
        mesh=mesh,
        in_specs=(P("gx", "az", "ta"), P("gx", "az", "ta"), P()),
        out_specs=P(("gx", "az", "ta"), None, None),
        check_vma=False,
    )
```
